512 devices in a mesh: ctx: 64 (over x, z, core), tp: 8 (over y).
Axes of the slice: x: 4, y: 8, z: 8, core: 2. Of those that a mesh axis runs over, the one named last changes fastest.
Arguments:
- hyena_q: bfloat16 [8192, 8192], P('ctx', 'tp'), may hold values from -36 to 36
- hyena_k: bfloat16 [8192, 8192], P('ctx', 'tp'), may hold values from -6 to 6
- hyena_v: bfloat16 [8192, 8192], P('ctx', 'tp'), may hold values from -6 to 6
- filter_rate: float32 [8192, 16], P('tp'), may hold values from 0 to 1, as said below
- filter_residue: float32 [8192, 16], P('tp'), may hold values from -0.12 to 0.12
- skip_gain: float32 [8192], P('tp'), may hold values from 0.5 to 1.5
Outputs:
- hyena_out: bfloat16 [8192, 8192], P('ctx', 'tp')
The draws below stay inside these ranges and needn't reach their ends.
Inputs may be any that keep to these rules, and one draw needn't show every extreme that they name: `filter_rate`: every rate is positive and at most 0.05.
All inputs are finite; a program needn't handle non-finite values.
Results may differ from the reference program's by a relative error of at most 0.0057.
Values may be sent and summed in bfloat16 or wider, within the bound.
No kernel may reach another device: no remote copies, remote signals or barrier semaphores. Data moves between devices by JAX's collectives and lax.ppermute only.
A program may use at most 64 MiB of HBM per device.

```python
import jax
import jax.numpy as jnp
from jax import lax

D = 8192
ORDER = 16
SEQ = 8192


def draw_hyena_q(key, part):
    base = jax.random.fold_in(key, 77)
    key_a = jax.random.fold_in(base, 0)
    key_c = jax.random.fold_in(base, 2)
    columns = jnp.arange(D, dtype=jnp.float32) / (D - 1)
    chan_scale = 0.3 * jnp.exp(columns * jnp.log(10.0))
    row_scale = 0.3 * jnp.exp(jax.random.uniform(key_a, (SEQ,), jnp.float32) * jnp.log(10.0))
    values = jnp.clip(jax.random.normal(key_c, (SEQ, D), jnp.float32), -4.0, 4.0)
    return (values * row_scale[:, None] * chan_scale[None, :]).astype(jnp.bfloat16)


def draw_filter_rate(key, part):
    base = jax.random.fold_in(key, 31)
    key_a = jax.random.fold_in(base, 0)
    slowest = jnp.log(0.5 / SEQ)
    fastest = jnp.log(0.05)
    level = jax.random.uniform(key_a, (D, ORDER), jnp.float32)
    return jnp.exp(slowest + level * (fastest - slowest))


def levels(own_key, dims, pieces, smallest, top_value):
    def one(dim, blocks):
        draws = jax.random.uniform(jax.random.fold_in(jax.random.fold_in(own_key, 6), dim), (blocks,), jnp.float32, smallest / len(pieces), top_value / len(pieces))
        return jnp.repeat(jnp.exp(draws), dims[dim] // blocks).reshape((-1,) + (1,) * (len(dims) - dim - 1))

    gain = one(*pieces[0])
    for cut in pieces[1:]:
        gain = gain * one(*cut)
    return gain


def noise(stream_key, shape, scale, limit, shards=(), kind=jnp.bfloat16):
    array = jax.random.normal(stream_key, shape, jnp.float32) * scale
    if len(shards) > 0:
        array = levels(stream_key, shape, shards, -0.22, 0.18) * array
    return jnp.clip(array, min=-limit, max=limit).astype(kind)


def setup_inputs(seed: int = 0) -> dict:
    seeds = jax.random.split(jax.random.key(seed), 7)
    return {
        "hyena_q": draw_hyena_q(jax.random.fold_in(seeds[6], 71), 0),
        "hyena_k": noise(seeds[1], (SEQ, D), 1.0, 6.0, ((0, 64), (1, 8))),
        "hyena_v": noise(seeds[2], (SEQ, D), 1.0, 6.0, ((0, 64), (1, 8))),
        "filter_rate": draw_filter_rate(jax.random.fold_in(seeds[6], 71), 0),
        "filter_residue": noise(seeds[4], (D, ORDER), 0.02, 0.12, ((0, 8),), jnp.float32),
        "skip_gain": jnp.clip(0.5 + 1.0 * jax.random.uniform(seeds[5], (D,), jnp.float32) ** levels(seeds[5], (D,), ((0, 8),), -0.2, 0.2), 0.5, 1.5),
    }


def reference(hyena_q, hyena_k, hyena_v, filter_rate, filter_residue, skip_gain):
    product = (hyena_k.astype(jnp.float32) * hyena_v.astype(jnp.float32)).astype(jnp.bfloat16)
    steps = jnp.arange(SEQ, dtype=jnp.float32)
    filters = jnp.zeros((D, SEQ), jnp.float32)
    for mode in range(ORDER):
        filters = filters + filter_residue[:, mode:mode + 1] * jnp.exp(-filter_rate[:, mode:mode + 1] * steps[None, :])
    length = 2 * SEQ
    spectrum = jnp.fft.rfft(product.astype(jnp.float32).T, n=length, axis=1) * jnp.fft.rfft(filters, n=length, axis=1)
    convolved = jnp.fft.irfft(spectrum, n=length, axis=1)[:, :SEQ].T
    gated = (hyena_q.astype(jnp.float32) * (convolved + skip_gain[None, :] * product.astype(jnp.float32))).astype(jnp.bfloat16)
    gated_wide = gated.astype(jnp.float32)
    sumsq = lax.optimization_barrier(jnp.sum(gated_wide * gated_wide, axis=1, keepdims=True))
    return (gated_wide / jnp.sqrt(sumsq / D + 1e-06)).astype(jnp.bfloat16)
```

```python
import functools

import jax
import jax.numpy as jnp
from jax import lax
from jax.experimental import pallas as pl
from jax.experimental.pallas import tpu as pltpu
from jax.sharding import PartitionSpec as P

ORDER = 16
LANES = 128
SUBS = 8


def vmem_call(kernel, out_shape, scratch=(), name=None):
    return pl.pallas_call(
        kernel,
        out_shape=out_shape,
        scratch_shapes=scratch,
        name=name,
        compiler_params=pltpu.CompilerParams(vmem_limit_bytes=48 * 1024 * 1024),
    )


def fill_product(k_ref, v_ref, u_ref):
    tokens, width = k_ref.shape
    groups = width // LANES
    for pair in range(tokens // 16):
        for g in range(groups):
            rows, cols = pl.ds(pair * 16, 16), pl.ds(g * LANES, LANES)
            k = k_ref[rows, cols].astype(jnp.float32)
            v = v_ref[rows, cols].astype(jnp.float32)
            p = (k * v).astype(jnp.bfloat16).astype(jnp.float32)
            u_ref[pl.ds((2 * pair * groups + g) * SUBS, SUBS), :] = p[:SUBS]
            u_ref[pl.ds(((2 * pair + 1) * groups + g) * SUBS, SUBS), :] = p[SUBS:]


def fill_modes(src_ref, dst_ref, fn):
    groups = src_ref.shape[0] // LANES
    for g in range(groups):
        part = src_ref[pl.ds(g * LANES, LANES), :].T
        dst_ref[pl.ds(g, ORDER, stride=groups), :] = fn(part)


def state_kernel(k_ref, v_ref, rate_ref, end_ref, u_ref, q_ref):
    fill_modes(rate_ref, q_ref, lambda r: jnp.exp(-r))
    fill_product(k_ref, v_ref, u_ref)
    blocks = k_ref.shape[0] // SUBS

    def step(tb, xs):
        for i in range(SUBS):
            u = u_ref[pl.ds(tb * 64 + i, SUBS, stride=SUBS), :]
            xs = tuple(
                q_ref[pl.ds(m * SUBS, SUBS), :] * xs[m] + u for m in range(ORDER)
            )
        return xs

    zero = jnp.zeros((SUBS, LANES), jnp.float32)
    xs = lax.fori_loop(0, blocks, step, (zero,) * ORDER)
    for m in range(ORDER):
        end_ref[pl.ds(m * SUBS, SUBS), :] = xs[m]


def local_kernel(k_ref, v_ref, rate_ref, res_ref, skip_ref, z_ref, e_ref, q8_ref, u_ref, q_ref, r_ref):
    fill_modes(rate_ref, q_ref, lambda r: jnp.exp(-r))
    fill_modes(res_ref, r_ref, lambda r: r)
    fill_product(k_ref, v_ref, u_ref)
    blocks = k_ref.shape[0] // SUBS
    for m in range(ORDER):
        rows = pl.ds(m * SUBS, SUBS)
        q = q_ref[rows, :]
        w = r_ref[rows, :] * q
        for i in range(SUBS):
            e_ref[pl.ds(m * 64 + i, SUBS, stride=SUBS), :] = w
            w = w * q
        q2 = q * q
        q4 = q2 * q2
        q8_ref[rows, :] = q4 * q4

    def step(tb, xs):
        for i in range(SUBS):
            u = u_ref[pl.ds(tb * 64 + i, SUBS, stride=SUBS), :]
            z = skip_ref[...] * u
            new = []
            for m in range(ORDER):
                rows = pl.ds(m * SUBS, SUBS)
                x = q_ref[rows, :] * xs[m] + u
                z = z + r_ref[rows, :] * x
                new.append(x)
            xs = tuple(new)
            z_ref[pl.ds(tb * 64 + i, SUBS, stride=SUBS), :] = z
        return xs

    zero = jnp.zeros((SUBS, LANES), jnp.float32)
    lax.fori_loop(0, blocks, step, (zero,) * ORDER)


def scan_kernel(rate_ref, end_ref, start_ref):
    rows = rate_ref.shape[0]
    decay = jnp.exp(-float(LANES) * rate_ref[...])
    x = jnp.zeros((rows, LANES), jnp.float32)
    blocks = end_ref.shape[0] // rows
    for b in range(blocks):
        start_ref[pl.ds(b * rows, rows), :] = x
        if b < blocks - 1:
            x = decay * x + end_ref[pl.ds(b * rows, rows), :]


def gate_kernel(q_ref, z_ref, e_ref, q8_ref, s_ref, gated_ref, sums_ref, sq_ref):
    tokens, width = q_ref.shape
    groups = width // LANES
    for g in range(groups):
        vs, decays = [], []
        for m in range(ORDER):
            row = pl.ds(m * groups + g, 1)
            s = jnp.broadcast_to(s_ref[row, :], (SUBS, LANES))
            vs.append(s * e_ref[pl.ds((m * groups + g) * SUBS, SUBS), :])
            decays.append(jnp.broadcast_to(q8_ref[row, :], (SUBS, LANES)))
        for pair in range(tokens // 16):
            parts = []
            for half in range(2):
                tb = 2 * pair + half
                parts.append(z_ref[pl.ds((tb * groups + g) * SUBS, SUBS), :] + functools.reduce(jnp.add, vs))
                vs = [v * d for v, d in zip(vs, decays)]
            rows, cols = pl.ds(pair * 16, 16), pl.ds(g * LANES, LANES)
            wide = q_ref[rows, cols].astype(jnp.float32) * jnp.concatenate(parts, axis=0)
            gated = wide.astype(jnp.bfloat16)
            gated_ref[rows, cols] = gated
            square = gated.astype(jnp.float32)
            square = square * square
            if g == 0:
                sq_ref[rows, :] = square
            else:
                sq_ref[rows, :] = sq_ref[rows, :] + square
    sums_ref[...] = lax.dot_general(
        jnp.ones((SUBS, LANES), jnp.float32),
        sq_ref[...],
        (((1,), (1,)), ((), ())),
        precision=lax.Precision.HIGHEST,
        preferred_element_type=jnp.float32,
    )


def norm_kernel(scale, sums_ref, gated_ref, out_ref):
    tokens, width = gated_ref.shape
    total = lax.dot_general(
        sums_ref[...],
        jnp.ones((SUBS, LANES), jnp.float32),
        (((0,), (0,)), ((), ())),
        precision=lax.Precision.HIGHEST,
        preferred_element_type=jnp.float32,
    )
    inv = 1.0 / jnp.sqrt(total * scale + 1e-06)
    for g in range(width // LANES):
        cols = pl.ds(g * LANES, LANES)
        out_ref[:, cols] = (gated_ref[:, cols].astype(jnp.float32) * inv).astype(jnp.bfloat16)


def per_device(hyena_q, hyena_k, hyena_v, filter_rate, filter_residue, skip_gain):
    n_ctx = lax.axis_size("ctx")
    n_tp = lax.axis_size("tp")
    tokens, width = hyena_q.shape
    groups = width // LANES
    f32 = jnp.float32
    state = jax.ShapeDtypeStruct((ORDER * groups, LANES), f32)
    table = jax.ShapeDtypeStruct((tokens * groups, LANES), f32)
    plane = pltpu.VMEM((tokens * groups, LANES), f32)
    small = pltpu.VMEM((ORDER * groups, LANES), f32)

    ends = vmem_call(state_kernel, state, (plane, small), "states")(hyena_k, hyena_v, filter_rate)
    rows = ORDER * groups // n_ctx
    gathered = lax.all_to_all(
        ends.reshape(n_ctx, rows, LANES), "ctx", split_axis=0, concat_axis=0, tiled=True
    )
    z, e, q8 = vmem_call(
        local_kernel, (table, jax.ShapeDtypeStruct((ORDER * groups * SUBS, LANES), f32), state),
        (plane, small, small), "local",
    )(hyena_k, hyena_v, filter_rate, filter_residue, skip_gain.reshape(groups, LANES))
    rates = filter_rate.T.reshape(ORDER * groups, LANES)
    my_rates = lax.dynamic_slice_in_dim(rates, lax.axis_index("ctx") * rows, rows, 0)
    starts = vmem_call(scan_kernel, state, (), "scan")(
        my_rates, gathered.reshape(ORDER * groups, LANES)
    )
    carried = lax.all_to_all(
        starts.reshape(n_ctx, rows, LANES), "ctx", split_axis=0, concat_axis=0, tiled=True
    )
    gated, sums = vmem_call(
        gate_kernel,
        (jax.ShapeDtypeStruct((tokens, width), jnp.bfloat16), jax.ShapeDtypeStruct((n_tp, tokens), f32)),
        (pltpu.VMEM((tokens, LANES), f32),), "gate",
    )(hyena_q, z, e, q8, carried.reshape(ORDER * groups, LANES))
    all_sums = lax.all_to_all(sums, "tp", split_axis=0, concat_axis=0, tiled=True)
    return vmem_call(
        functools.partial(norm_kernel, 1.0 / (n_tp * width)),
        jax.ShapeDtypeStruct((tokens, width), jnp.bfloat16), (), "norm",
    )(all_sums, gated)


def solution(mesh):
    in_specs = (
        P("ctx", "tp"),
        P("ctx", "tp"),
        P("ctx", "tp"),
        P("tp", None),
        P("tp", None),
        P("tp"),
    )
    return jax.shard_map(
        per_device, mesh=mesh, in_specs=in_specs, out_specs=P("ctx", "tp"), check_vma=False
    )
```

```python
import functools

import jax
import jax.numpy as jnp
from jax import lax
from jax.experimental import pallas as pl
from jax.experimental.pallas import tpu as pltpu
from jax.sharding import PartitionSpec as P

ORDER = 16
LANES = 128
SUBS = 8
CORES = 2
RINGS = 8
Z_TYPE = jnp.float32
X_TYPE = jnp.float32


def call(kernel, out_shape, scratch=(), name=None, ins=None, outs=None):
    specs = {}
    if ins is not None:
        specs["in_specs"] = [pl.BlockSpec(memory_space=space) for space in ins]
    if outs is not None:
        specs["out_specs"] = pl.BlockSpec(memory_space=outs)
    return pl.pallas_call(
        kernel,
        out_shape=out_shape,
        scratch_shapes=scratch,
        name=name,
        compiler_params=pltpu.CompilerParams(vmem_limit_bytes=48 * 1024 * 1024),
        **specs,
    )


def fill_modes(src_ref, dst_ref, fn):
    groups = src_ref.shape[1] // LANES
    for g in range(groups):
        dst_ref[pl.ds(g, ORDER, stride=groups), :] = fn(src_ref[:, pl.ds(g * LANES, LANES)])


def state_kernel(k_hbm, v_hbm, rate_hbm, end_ref, u_ref, rows_ref, k_ref, v_ref, rate_ref, q_ref, sems, rate_sem):
    tokens, width = k_ref.shape
    groups = width // LANES
    pairs = tokens // 16

    def fetch(pair):
        rows = pl.ds(pair * 16, 16)
        return (
            pltpu.make_async_copy(k_hbm.at[rows, :], k_ref.at[rows, :], sems.at[0, pair]),
            pltpu.make_async_copy(v_hbm.at[rows, :], v_ref.at[rows, :], sems.at[1, pair]),
        )

    rates = pltpu.make_async_copy(rate_hbm, rate_ref, rate_sem)
    rates.start()
    for pair in range(pairs):
        for copy in fetch(pair):
            copy.start()
    rates.wait()
    fill_modes(rate_ref, rows_ref, lambda r: r)
    fill_modes(rate_ref, q_ref, lambda r: jnp.exp(-r))
    qs = tuple(q_ref[pl.ds(m * groups, groups), :] for m in range(ORDER))
    xs = (jnp.zeros((SUBS, LANES), jnp.float32),) * ORDER
    for pair in range(pairs):
        for copy in fetch(pair):
            copy.wait()
        rows = pl.ds(pair * 16, 16)
        for g in range(groups):
            cols = pl.ds(g * LANES, LANES)
            p = k_ref[rows, cols].astype(jnp.float32) * v_ref[rows, cols].astype(jnp.float32)
            p = p.astype(jnp.bfloat16).astype(jnp.float32)
            u_ref[pl.ds((2 * pair * groups + g) * SUBS, SUBS), :] = p[:SUBS]
            u_ref[pl.ds(((2 * pair + 1) * groups + g) * SUBS, SUBS), :] = p[SUBS:]

        def step(tb, xs):
            for i in range(SUBS):
                u = u_ref[pl.ds(tb * groups * SUBS + i, groups, stride=SUBS), :]
                xs = tuple(q * x + u for q, x in zip(qs, xs))
            return xs

        xs = lax.fori_loop(2 * pair, 2 * pair + 2, step, xs)
    for m in range(ORDER):
        end_ref[pl.ds(m * groups, groups), :] = xs[m]


def local_kernel(u_ref, rate_ref, res_ref, skip_ref, z_ref, e_ref, q8_ref, q_ref, r_ref):
    q_ref[...] = jnp.exp(-rate_ref[...])
    fill_modes(res_ref, r_ref, lambda r: r)
    for m in range(ORDER):
        rows = pl.ds(m * SUBS, SUBS)
        q = q_ref[rows, :]
        w = r_ref[rows, :] * q
        for i in range(SUBS):
            e_ref[pl.ds(m * 64 + i, SUBS, stride=SUBS), :] = w
            w = w * q
        q2 = q * q
        q4 = q2 * q2
        q8_ref[rows, :] = q4 * q4

    def step(tb, xs):
        for i in range(SUBS):
            u = u_ref[pl.ds(tb * 64 + i, SUBS, stride=SUBS), :]
            z = skip_ref[...] * u
            new = []
            for m in range(ORDER):
                rows = pl.ds(m * SUBS, SUBS)
                x = q_ref[rows, :] * xs[m] + u
                z = z + r_ref[rows, :] * x
                new.append(x)
            xs = tuple(new)
            z_ref[pl.ds(tb * 64 + i, SUBS, stride=SUBS), :] = z
        return xs

    zero = jnp.zeros((SUBS, LANES), jnp.float32)
    lax.fori_loop(0, u_ref.shape[0] // 64, step, (zero,) * ORDER)


def decay_of(rate, positions):
    return jnp.exp(rate * -positions)


def half_rates(rate_ref):
    half = rate_ref.shape[0] // CORES
    core = lax.axis_index("ctx") % CORES
    return pl.ds(pl.multiple_of(core * half, SUBS), half)


def chip_kernel(rate_ref, ends_ref, total_ref):
    rows = half_rates(rate_ref)
    decay = decay_of(rate_ref[rows, :], float(LANES))
    total = (decay * ends_ref[0, rows, :] + ends_ref[1, rows, :]).astype(total_ref.dtype)
    for copy in range(total_ref.shape[0]):
        total_ref[copy] = total


def prefix(part, count, decay, place):
    run = jnp.zeros(decay.shape, jnp.float32)
    before = run
    for n in range(count):
        before = jnp.where(place == n, run, before)
        run = decay * run + part(n).astype(jnp.float32)
    return before, run


def ring_kernel(rate_ref, totals_ref, before_ref, wholes_ref):
    place = lax.axis_index("ctx") // CORES % RINGS
    decay = decay_of(rate_ref[half_rates(rate_ref), :], float(CORES * LANES))
    before, run = prefix(lambda n: totals_ref[n], RINGS, decay, place)
    before_ref[...] = before
    whole = run.astype(wholes_ref.dtype)
    for copy in range(wholes_ref.shape[0]):
        wholes_ref[copy] = whole


def start_kernel(rate_ref, wholes_ref, before_ref, ends_ref, start_ref):
    me = lax.axis_index("ctx")
    x, z = me // (CORES * RINGS), me // CORES % RINGS
    rows = half_rates(rate_ref)
    rate = rate_ref[rows, :]
    far, _ = prefix(
        lambda n: wholes_ref[n], wholes_ref.shape[0], decay_of(rate, float(RINGS * CORES * LANES)), x
    )
    first = decay_of(rate, float(CORES * LANES) * z.astype(jnp.float32)) * far + before_ref[...]
    start_ref[0] = first
    start_ref[1] = decay_of(rate, float(LANES)) * first + ends_ref[0, rows, :]


def gate_kernel(q_ref, z_ref, e_ref, q8_ref, starts_ref, gated_ref, sums_ref, sq_ref):
    core = lax.axis_index("ctx") % CORES
    n_rows = starts_ref.shape[2]
    tokens, width = q_ref.shape
    groups = width // LANES
    for g in range(groups):
        vs, decays = [], []
        for m in range(ORDER):
            at = m * groups + g
            row = pl.ds(at, 1)
            s = starts_ref[at // n_rows, core, pl.ds(at % n_rows, 1), :]
            s = jnp.broadcast_to(s, (SUBS, LANES))
            vs.append(s * e_ref[pl.ds((m * groups + g) * SUBS, SUBS), :])
            decays.append(jnp.broadcast_to(q8_ref[row, :], (SUBS, LANES)))
        for pair in range(tokens // 16):
            parts = []
            for half in range(2):
                tb = 2 * pair + half
                parts.append(z_ref[pl.ds((tb * groups + g) * SUBS, SUBS), :] + functools.reduce(jnp.add, vs))
                vs = [v * d for v, d in zip(vs, decays)]
            rows, cols = pl.ds(pair * 16, 16), pl.ds(g * LANES, LANES)
            wide = q_ref[rows, cols].astype(jnp.float32) * jnp.concatenate(parts, axis=0)
            gated = wide.astype(jnp.bfloat16)
            gated_ref[rows, cols] = gated
            square = gated.astype(jnp.float32)
            square = square * square
            if g == 0:
                sq_ref[rows, :] = square
            else:
                sq_ref[rows, :] = sq_ref[rows, :] + square
    sums_ref[...] = lax.dot_general(
        jnp.ones((SUBS, LANES), jnp.float32),
        sq_ref[...],
        (((1,), (1,)), ((), ())),
        precision=lax.Precision.HIGHEST,
        preferred_element_type=jnp.float32,
    )


def norm_kernel(scale, sums_ref, gated_ref, out_hbm, out_ref, sems):
    tokens, width = gated_ref.shape
    chunks = sems.shape[0]
    total = lax.dot_general(
        sums_ref[...],
        jnp.ones((sums_ref.shape[0], LANES), jnp.float32),
        (((0,), (0,)), ((), ())),
        precision=lax.Precision.HIGHEST,
        preferred_element_type=jnp.float32,
    )
    inv = 1.0 / jnp.sqrt(total * scale + 1e-06)
    copies = []
    for chunk in range(chunks):
        size = tokens // chunks
        rows = pl.ds(chunk * size, size)
        part = inv[chunk * size:(chunk + 1) * size]
        for g in range(width // LANES):
            cols = pl.ds(g * LANES, LANES)
            out_ref[rows, cols] = (gated_ref[rows, cols].astype(jnp.float32) * part).astype(jnp.bfloat16)
        copies.append(pltpu.make_async_copy(out_ref.at[rows, :], out_hbm.at[rows, :], sems.at[chunk]))
        copies[-1].start()
    for copy in copies:
        copy.wait()


def per_device(hyena_q, hyena_k, hyena_v, filter_rate, filter_residue, skip_gain):
    n_ctx = lax.axis_size("ctx")
    n_tp = lax.axis_size("tp")
    tokens, width = hyena_q.shape
    groups = width // LANES
    f32, bf16 = jnp.float32, jnp.bfloat16
    rows = ORDER * groups
    half = rows // CORES
    shape = jax.ShapeDtypeStruct
    state = shape((rows, LANES), f32)
    table = shape((tokens * groups, LANES), f32)
    small = pltpu.VMEM((rows, LANES), f32)
    tile = pltpu.VMEM((tokens, width), bf16)
    n_x = n_ctx // (CORES * RINGS)
    pairs = [[CORES * i + c for c in range(CORES)] for i in range(n_ctx // CORES)]
    along_z = [
        [(x * RINGS + z) * CORES + c for z in range(RINGS)] for x in range(n_x) for c in range(CORES)
    ]
    along_x = [[x * RINGS * CORES + r for x in range(n_x)] for r in range(RINGS * CORES)]

    def swap(array, places):
        return lax.all_to_all(
            array, "ctx", split_axis=0, concat_axis=0, tiled=True, axis_index_groups=places
        )

    rate = filter_rate.T
    ends, u, rate_rows = call(
        state_kernel, (state, table, state),
        (tile, tile, pltpu.VMEM((ORDER, width), f32), small,
         pltpu.SemaphoreType.DMA((2, tokens // 16)), pltpu.SemaphoreType.DMA),
        "states", (pl.ANY,) * 3,
    )(*(pltpu.with_memory_space_constraint(a, pltpu.HBM) for a in (hyena_k, hyena_v, rate)))
    ends = lax.all_gather(ends, "ctx", axis_index_groups=pairs)
    totals = call(chip_kernel, shape((RINGS, half, LANES), Z_TYPE), (), "chip")(rate_rows, ends)
    totals = swap(totals, along_z)
    before, wholes = call(
        ring_kernel, (shape((half, LANES), f32), shape((n_x, half, LANES), X_TYPE)), (), "ring",
    )(rate_rows, totals)
    wholes = swap(wholes, along_x)
    starts = call(start_kernel, shape((CORES, half, LANES), f32), (), "start")(rate_rows, wholes, before, ends)
    starts = lax.all_gather(starts, "ctx", axis_index_groups=pairs)
    z, e, q8 = call(
        local_kernel, (table, shape((rows * SUBS, LANES), f32), state), (small, small), "local",
    )(u, rate_rows, filter_residue.T, skip_gain.reshape(groups, LANES))
    gated, sums = call(
        gate_kernel,
        (shape((tokens, width), bf16), shape((n_tp, tokens), f32)),
        (pltpu.VMEM((tokens, LANES), f32),), "gate",
    )(hyena_q, z, e, q8, starts)
    all_sums = lax.all_to_all(sums, "tp", split_axis=0, concat_axis=0, tiled=True)
    return call(
        functools.partial(norm_kernel, 1.0 / (n_tp * width)),
        shape((tokens, width), bf16), (tile, pltpu.SemaphoreType.DMA((4,))), "norm",
        (pltpu.VMEM,) * 2, pltpu.HBM,
    )(all_sums, gated)


def solution(mesh):
    in_specs = (
        P("ctx", "tp"),
        P("ctx", "tp"),
        P("ctx", "tp"),
        P("tp", None),
        P("tp", None),
        P("tp"),
    )
    return jax.shard_map(
        per_device, mesh=mesh, in_specs=in_specs, out_specs=P("ctx", "tp"), check_vma=False
    )
```

```python
import functools

import jax
import jax.numpy as jnp
from jax import lax
from jax.experimental import pallas as pl
from jax.experimental.pallas import tpu as pltpu
from jax.sharding import PartitionSpec as P

ORDER = 16
LANES = 128
SUBS = 8
CORES = 2
RINGS = 8
CHUNKS = 4
Z_TYPE = jnp.bfloat16
X_TYPE = jnp.float32


def call(kernel, out_shape, scratch=(), name=None, ins=None, outs=None):
    specs = {}
    if ins is not None:
        specs["in_specs"] = [pl.BlockSpec(memory_space=space) for space in ins]
    if outs is not None:
        specs["out_specs"] = pl.BlockSpec(memory_space=outs)
    return pl.pallas_call(
        kernel,
        out_shape=out_shape,
        scratch_shapes=scratch,
        name=name,
        compiler_params=pltpu.CompilerParams(vmem_limit_bytes=48 * 1024 * 1024),
        **specs,
    )


def fill_modes(src_ref, dst_ref, fn):
    groups = src_ref.shape[1] // LANES
    for g in range(groups):
        dst_ref[pl.ds(g, ORDER, stride=groups), :] = fn(src_ref[:, pl.ds(g * LANES, LANES)])


def state_kernel(
    k_hbm, v_hbm, rate_hbm, res_hbm, skip_hbm, end_ref, z_ref, e_ref, q8_ref, rate_rows_ref,
    k_ref, v_ref, rate_ref, res_ref, skip_ref, u_ref, q_ref, r_ref, sems, mode_sems,
):
    tokens, width = k_ref.shape
    groups = width // LANES
    chunks = sems.shape[1]
    size = tokens // chunks

    def fetch(chunk):
        rows = pl.ds(chunk * size, size)
        return (
            pltpu.make_async_copy(k_hbm.at[rows, :], k_ref.at[rows, :], sems.at[0, chunk]),
            pltpu.make_async_copy(v_hbm.at[rows, :], v_ref.at[rows, :], sems.at[1, chunk]),
        )

    modes = (
        pltpu.make_async_copy(rate_hbm, rate_ref, mode_sems.at[0]),
        pltpu.make_async_copy(res_hbm, res_ref, mode_sems.at[1]),
        pltpu.make_async_copy(skip_hbm, skip_ref, mode_sems.at[2]),
    )
    for copy in modes:
        copy.start()
    for chunk in range(chunks):
        for copy in fetch(chunk):
            copy.start()
    for copy in modes:
        copy.wait()
    fill_modes(rate_ref, rate_rows_ref, lambda r: r)
    fill_modes(res_ref, r_ref, lambda r: r)
    q_ref[...] = jnp.exp(-rate_rows_ref[...])
    for m in range(ORDER):
        rows = pl.ds(m * groups, groups)
        q = q_ref[rows, :]
        w = r_ref[rows, :] * q
        for i in range(SUBS):
            e_ref[pl.ds(m * groups * SUBS + i, groups, stride=SUBS), :] = w
            w = w * q
        q2 = q * q
        q4 = q2 * q2
        q8_ref[rows, :] = q4 * q4
    xs = (jnp.zeros((SUBS, LANES), jnp.float32),) * ORDER
    for chunk in range(chunks):
        for copy in fetch(chunk):
            copy.wait()
        for pair in range(chunk * size // 16, (chunk + 1) * size // 16):
            rows = pl.ds(pair * 16, 16)
            for g in range(groups):
                cols = pl.ds(g * LANES, LANES)
                p = k_ref[rows, cols].astype(jnp.float32) * v_ref[rows, cols].astype(jnp.float32)
                p = p.astype(jnp.bfloat16).astype(jnp.float32)
                u_ref[pl.ds((2 * pair * groups + g) * SUBS, SUBS), :] = p[:SUBS]
                u_ref[pl.ds(((2 * pair + 1) * groups + g) * SUBS, SUBS), :] = p[SUBS:]

        def step(tb, xs):
            for i in range(SUBS):
                at = pl.ds(tb * groups * SUBS + i, groups, stride=SUBS)
                u = u_ref[at, :]
                terms, new = [skip_ref[...] * u], []
                for m in range(ORDER):
                    rows = pl.ds(m * groups, groups)
                    x = q_ref[rows, :] * xs[m] + u
                    terms.append(r_ref[rows, :] * x)
                    new.append(x)
                xs = tuple(new)
                while len(terms) > 1:
                    terms = [functools.reduce(jnp.add, terms[n:n + 2]) for n in range(0, len(terms), 2)]
                z_ref[at, :] = terms[0]
            return xs

        xs = lax.fori_loop(chunk * size // SUBS, (chunk + 1) * size // SUBS, step, xs)
    for m in range(ORDER):
        end_ref[pl.ds(m * groups, groups), :] = xs[m]


def decay_of(rate, positions):
    return jnp.exp(rate * -positions)


def half_rates(rate_ref):
    half = rate_ref.shape[0] // CORES
    core = lax.axis_index("ctx") % CORES
    return pl.ds(pl.multiple_of(core * half, SUBS), half)


def chip_kernel(rate_ref, ends_ref, total_ref):
    rows = half_rates(rate_ref)
    decay = decay_of(rate_ref[rows, :], float(LANES))
    total = (decay * ends_ref[0, rows, :] + ends_ref[1, rows, :]).astype(total_ref.dtype)
    for copy in range(total_ref.shape[0]):
        total_ref[copy] = total


def prefix(part, count, decay, place):
    run = jnp.zeros(decay.shape, jnp.float32)
    before = run
    for n in range(count):
        before = jnp.where(place == n, run, before)
        run = decay * run + part(n).astype(jnp.float32)
    return before, run


def ring_kernel(rate_ref, totals_ref, before_ref, wholes_ref):
    place = lax.axis_index("ctx") // CORES % RINGS
    decay = decay_of(rate_ref[half_rates(rate_ref), :], float(CORES * LANES))
    before, run = prefix(lambda n: totals_ref[n], RINGS, decay, place)
    before_ref[...] = before
    whole = run.astype(wholes_ref.dtype)
    for copy in range(wholes_ref.shape[0]):
        wholes_ref[copy] = whole


def start_kernel(rate_ref, wholes_ref, before_ref, ends_ref, start_ref):
    me = lax.axis_index("ctx")
    x, z = me // (CORES * RINGS), me // CORES % RINGS
    rows = half_rates(rate_ref)
    rate = rate_ref[rows, :]
    far, _ = prefix(
        lambda n: wholes_ref[n], wholes_ref.shape[0], decay_of(rate, float(RINGS * CORES * LANES)), x
    )
    first = decay_of(rate, float(CORES * LANES) * z.astype(jnp.float32)) * far + before_ref[...]
    start_ref[0] = first
    start_ref[1] = decay_of(rate, float(LANES)) * first + ends_ref[0, rows, :]


def gate_kernel(q_ref, z_ref, e_ref, q8_ref, starts_ref, gated_ref, sums_ref, sq_ref):
    core = lax.axis_index("ctx") % CORES
    n_rows = starts_ref.shape[2]
    tokens, width = q_ref.shape
    groups = width // LANES
    for g in range(groups):
        vs, decays = [], []
        for m in range(ORDER):
            at = m * groups + g
            row = pl.ds(at, 1)
            s = starts_ref[at // n_rows, core, pl.ds(at % n_rows, 1), :]
            s = jnp.broadcast_to(s, (SUBS, LANES))
            vs.append(s * e_ref[pl.ds((m * groups + g) * SUBS, SUBS), :])
            decays.append(jnp.broadcast_to(q8_ref[row, :], (SUBS, LANES)))
        for pair in range(tokens // 16):
            parts = []
            for half in range(2):
                tb = 2 * pair + half
                parts.append(z_ref[pl.ds((tb * groups + g) * SUBS, SUBS), :] + functools.reduce(jnp.add, vs))
                vs = [v * d for v, d in zip(vs, decays)]
            rows, cols = pl.ds(pair * 16, 16), pl.ds(g * LANES, LANES)
            wide = q_ref[rows, cols].astype(jnp.float32) * jnp.concatenate(parts, axis=0)
            gated = wide.astype(jnp.bfloat16)
            gated_ref[rows, cols] = gated
            square = gated.astype(jnp.float32)
            square = square * square
            if g == 0:
                sq_ref[rows, :] = square
            else:
                sq_ref[rows, :] = sq_ref[rows, :] + square
    sums_ref[...] = lax.dot_general(
        jnp.ones((SUBS, LANES), jnp.float32),
        sq_ref[...],
        (((1,), (1,)), ((), ())),
        precision=lax.Precision.HIGHEST,
        preferred_element_type=jnp.float32,
    )


def norm_kernel(scale, sums_ref, gated_ref, out_hbm, out_ref, sems):
    tokens, width = gated_ref.shape
    chunks = sems.shape[0]
    total = lax.dot_general(
        sums_ref[...],
        jnp.ones((sums_ref.shape[0], LANES), jnp.float32),
        (((0,), (0,)), ((), ())),
        precision=lax.Precision.HIGHEST,
        preferred_element_type=jnp.float32,
    )
    inv = 1.0 / jnp.sqrt(total * scale + 1e-06)
    copies = []
    for chunk in range(chunks):
        size = tokens // chunks
        rows = pl.ds(chunk * size, size)
        part = inv[chunk * size:(chunk + 1) * size]
        for g in range(width // LANES):
            cols = pl.ds(g * LANES, LANES)
            out_ref[rows, cols] = (gated_ref[rows, cols].astype(jnp.float32) * part).astype(jnp.bfloat16)
        copies.append(pltpu.make_async_copy(out_ref.at[rows, :], out_hbm.at[rows, :], sems.at[chunk]))
        copies[-1].start()
    for copy in copies:
        copy.wait()


def per_device(hyena_q, hyena_k, hyena_v, filter_rate, filter_residue, skip_gain):
    n_ctx = lax.axis_size("ctx")
    n_tp = lax.axis_size("tp")
    tokens, width = hyena_q.shape
    groups = width // LANES
    f32, bf16 = jnp.float32, jnp.bfloat16
    rows = ORDER * groups
    half = rows // CORES
    shape = jax.ShapeDtypeStruct
    state = shape((rows, LANES), f32)
    table = shape((tokens * groups, LANES), f32)
    small = pltpu.VMEM((rows, LANES), f32)
    tile = pltpu.VMEM((tokens, width), bf16)
    n_x = n_ctx // (CORES * RINGS)
    pairs = [[CORES * i + c for c in range(CORES)] for i in range(n_ctx // CORES)]
    along_z = [
        [(x * RINGS + z) * CORES + c for z in range(RINGS)] for x in range(n_x) for c in range(CORES)
    ]
    along_x = [[x * RINGS * CORES + r for x in range(n_x)] for r in range(RINGS * CORES)]

    def swap(array, places):
        return lax.all_to_all(
            array, "ctx", split_axis=0, concat_axis=0, tiled=True, axis_index_groups=places
        )

    rate = filter_rate.T
    weights = shape((rows * SUBS, LANES), f32)
    modes = pltpu.VMEM((ORDER, width), f32)
    ends, z, e, q8, rate_rows = call(
        state_kernel, (state, table, weights, state, state),
        (tile, tile, modes, modes, pltpu.VMEM((groups, LANES), f32), pltpu.VMEM(table.shape, f32), small, small,
         pltpu.SemaphoreType.DMA((2, CHUNKS)), pltpu.SemaphoreType.DMA((3,))),
        "states", (pltpu.HBM,) * 5,
    )(*(
        pltpu.with_memory_space_constraint(array, pltpu.HBM)
        for array in (hyena_k, hyena_v, rate, filter_residue.T, skip_gain.reshape(groups, LANES))
    ))
    ends = lax.all_gather(ends, "ctx", axis_index_groups=pairs)
    totals = call(chip_kernel, shape((RINGS, half, LANES), Z_TYPE), (), "chip")(rate_rows, ends)
    totals = swap(totals, along_z)
    before, wholes = call(
        ring_kernel, (shape((half, LANES), f32), shape((n_x, half, LANES), X_TYPE)), (), "ring",
    )(rate_rows, totals)
    wholes = swap(wholes, along_x)
    starts = call(start_kernel, shape((CORES, half, LANES), f32), (), "start")(rate_rows, wholes, before, ends)
    starts = lax.all_gather(starts, "ctx", axis_index_groups=pairs)
    gated, sums = call(
        gate_kernel,
        (shape((tokens, width), bf16), shape((n_tp, tokens), f32)),
        (pltpu.VMEM((tokens, LANES), f32),), "gate",
    )(hyena_q, z, e, q8, starts)
    all_sums = lax.all_to_all(sums, "tp", split_axis=0, concat_axis=0, tiled=True)
    return call(
        functools.partial(norm_kernel, 1.0 / (n_tp * width)),
        shape((tokens, width), bf16), (tile, pltpu.SemaphoreType.DMA((4,))), "norm",
        (pltpu.VMEM,) * 2, pltpu.HBM,
    )(all_sums, gated)


def solution(mesh):
    in_specs = (
        P("ctx", "tp"),
        P("ctx", "tp"),
        P("ctx", "tp"),
        P("tp", None),
        P("tp", None),
        P("tp"),
    )
    return jax.shard_map(
        per_device, mesh=mesh, in_specs=in_specs, out_specs=P("ctx", "tp"), check_vma=False
    )
```

```python
import functools

import jax
import jax.numpy as jnp
from jax import lax
from jax.experimental import pallas as pl
from jax.experimental.pallas import tpu as pltpu
from jax.sharding import PartitionSpec as P

ORDER = 16
LANES = 128
SUBS = 8
CORES = 2
RINGS = 8
CHUNKS = 2
Z_TYPE = jnp.bfloat16
X_TYPE = jnp.bfloat16


def call(kernel, out_shape, scratch=(), name=None, ins=None, outs=None):
    specs = {}
    if ins is not None:
        specs["in_specs"] = [pl.BlockSpec(memory_space=space) for space in ins]
    if outs is not None:
        specs["out_specs"] = pl.BlockSpec(memory_space=outs)
    return pl.pallas_call(
        kernel,
        out_shape=out_shape,
        scratch_shapes=scratch,
        name=name,
        compiler_params=pltpu.CompilerParams(vmem_limit_bytes=48 * 1024 * 1024),
        **specs,
    )


def fill_modes(src_ref, dst_ref, fn):
    groups = src_ref.shape[1] // LANES
    for g in range(groups):
        dst_ref[pl.ds(g, ORDER, stride=groups), :] = fn(src_ref[:, pl.ds(g * LANES, LANES)])


def state_kernel(
    k_hbm, v_hbm, rate_hbm, res_hbm, skip_hbm, end_ref, z_ref, e_ref, q8_ref, rate_rows_ref,
    k_ref, v_ref, rate_ref, res_ref, skip_ref, u_ref, q_ref, r_ref, sems, mode_sems,
):
    tokens, width = k_ref.shape
    groups = width // LANES
    chunks = sems.shape[1]
    size = tokens // chunks

    def fetch(chunk):
        rows = pl.ds(chunk * size, size)
        return (
            pltpu.make_async_copy(k_hbm.at[rows, :], k_ref.at[rows, :], sems.at[0, chunk]),
            pltpu.make_async_copy(v_hbm.at[rows, :], v_ref.at[rows, :], sems.at[1, chunk]),
        )

    modes = (
        pltpu.make_async_copy(rate_hbm, rate_ref, mode_sems.at[0]),
        pltpu.make_async_copy(res_hbm, res_ref, mode_sems.at[1]),
        pltpu.make_async_copy(skip_hbm, skip_ref, mode_sems.at[2]),
    )
    for copy in modes:
        copy.start()
    for chunk in range(chunks):
        for copy in fetch(chunk):
            copy.start()
    for copy in modes:
        copy.wait()
    fill_modes(rate_ref, rate_rows_ref, lambda r: r)
    fill_modes(res_ref, r_ref, lambda r: r)
    q_ref[...] = jnp.exp(-rate_rows_ref[...])
    for m in range(ORDER):
        rows = pl.ds(m * groups, groups)
        q = q_ref[rows, :]
        w = r_ref[rows, :] * q
        for i in range(SUBS):
            e_ref[pl.ds(m * groups * SUBS + i, groups, stride=SUBS), :] = w
            w = w * q
        q2 = q * q
        q4 = q2 * q2
        q8_ref[rows, :] = q4 * q4
    rs = tuple(r_ref[pl.ds(m * groups, groups), :] for m in range(ORDER))
    qs = tuple(q_ref[pl.ds(m * groups, groups), :] for m in range(ORDER))
    xs = (jnp.zeros((SUBS, LANES), jnp.float32),) * ORDER
    for chunk in range(chunks):
        for copy in fetch(chunk):
            copy.wait()
        for pair in range(chunk * size // 16, (chunk + 1) * size // 16):
            rows = pl.ds(pair * 16, 16)
            for g in range(groups):
                cols = pl.ds(g * LANES, LANES)
                p = k_ref[rows, cols].astype(jnp.float32) * v_ref[rows, cols].astype(jnp.float32)
                p = p.astype(jnp.bfloat16).astype(jnp.float32)
                u_ref[pl.ds((2 * pair * groups + g) * SUBS, SUBS), :] = p[:SUBS]
                u_ref[pl.ds(((2 * pair + 1) * groups + g) * SUBS, SUBS), :] = p[SUBS:]

        def step(tb, xs):
            for i in range(SUBS):
                at = pl.ds(tb * groups * SUBS + i, groups, stride=SUBS)
                u = u_ref[at, :]
                terms, new = [skip_ref[...] * u], []
                for m in range(ORDER):
                    rows = pl.ds(m * groups, groups)
                    x = qs[m] * xs[m] + u
                    terms.append(rs[m] * x)
                    new.append(x)
                xs = tuple(new)
                while len(terms) > 1:
                    terms = [functools.reduce(jnp.add, terms[n:n + 2]) for n in range(0, len(terms), 2)]
                z_ref[at, :] = terms[0]
            return xs

        xs = lax.fori_loop(chunk * size // SUBS, (chunk + 1) * size // SUBS, step, xs)
    for m in range(ORDER):
        end_ref[pl.ds(m * groups, groups), :] = xs[m]


def decay_of(rate, positions):
    return jnp.exp(rate * -positions)


def half_rates(rate_ref):
    half = rate_ref.shape[0] // CORES
    core = lax.axis_index("ctx") % CORES
    return pl.ds(pl.multiple_of(core * half, SUBS), half)


def chip_kernel(rate_ref, ends_ref, total_ref):
    rows = half_rates(rate_ref)
    decay = decay_of(rate_ref[rows, :], float(LANES))
    total = (decay * ends_ref[0, rows, :] + ends_ref[1, rows, :]).astype(total_ref.dtype)
    for copy in range(total_ref.shape[0]):
        total_ref[copy] = total


def prefix(part, count, decay, place):
    run = jnp.zeros(decay.shape, jnp.float32)
    before = run
    for n in range(count):
        before = jnp.where(place == n, run, before)
        run = decay * run + part(n).astype(jnp.float32)
    return before, run


def ring_kernel(rate_ref, totals_ref, wholes_ref):
    me = lax.axis_index("ctx")
    decay = decay_of(rate_ref[half_rates(rate_ref), :], float(CORES * LANES))
    before, run = prefix(lambda n: totals_ref[n], RINGS, decay, me // CORES % RINGS)
    x = me // (CORES * RINGS)
    for n in range(wholes_ref.shape[0]):
        wholes_ref[n] = jnp.where(x == n // CORES, before, run).astype(wholes_ref.dtype)


def block_start(rate_ref, wholes_ref, ends_ref, s_ref):
    me = lax.axis_index("ctx")
    x, z, core = me // (CORES * RINGS), me // CORES % RINGS, me % CORES
    half = wholes_ref.shape[1]
    for h in range(CORES):
        rows = pl.ds(h * half, half)
        rate = rate_ref[rows, :]
        far, _ = prefix(
            lambda n: wholes_ref[n * CORES + h], wholes_ref.shape[0] // CORES,
            decay_of(rate, float(RINGS * CORES * LANES)), x,
        )
        near = wholes_ref[x * CORES + h].astype(jnp.float32)
        first = decay_of(rate, float(CORES * LANES) * z.astype(jnp.float32)) * far + near
        second = decay_of(rate, float(LANES)) * first + ends_ref[0, rows, :]
        s_ref[rows, :] = jnp.where(core == 0, first, second)


def gate_kernel(q_ref, z_ref, e_ref, q8_ref, rate_ref, wholes_ref, ends_ref, gated_ref, sums_ref, sq_ref, s_ref):
    block_start(rate_ref, wholes_ref, ends_ref, s_ref)
    tokens, width = q_ref.shape
    groups = width // LANES
    for g in range(groups):
        vs, decays = [], []
        for m in range(ORDER):
            row = pl.ds(m * groups + g, 1)
            s = jnp.broadcast_to(s_ref[row, :], (SUBS, LANES))
            vs.append(s * e_ref[pl.ds((m * groups + g) * SUBS, SUBS), :])
            decays.append(jnp.broadcast_to(q8_ref[row, :], (SUBS, LANES)))
        for pair in range(tokens // 16):
            parts = []
            for half in range(2):
                tb = 2 * pair + half
                parts.append(z_ref[pl.ds((tb * groups + g) * SUBS, SUBS), :] + functools.reduce(jnp.add, vs))
                vs = [v * d for v, d in zip(vs, decays)]
            rows, cols = pl.ds(pair * 16, 16), pl.ds(g * LANES, LANES)
            wide = q_ref[rows, cols].astype(jnp.float32) * jnp.concatenate(parts, axis=0)
            gated = wide.astype(jnp.bfloat16)
            gated_ref[rows, cols] = gated
            square = gated.astype(jnp.float32)
            square = square * square
            if g == 0:
                sq_ref[rows, :] = square
            else:
                sq_ref[rows, :] = sq_ref[rows, :] + square
    sums_ref[...] = lax.dot_general(
        jnp.ones((SUBS, LANES), jnp.float32),
        sq_ref[...],
        (((1,), (1,)), ((), ())),
        precision=lax.Precision.HIGHEST,
        preferred_element_type=jnp.float32,
    )


def norm_kernel(scale, sums_ref, gated_ref, out_hbm, out_ref, sems):
    tokens, width = gated_ref.shape
    chunks = sems.shape[0]
    total = lax.dot_general(
        sums_ref[...],
        jnp.ones((sums_ref.shape[0], LANES), jnp.float32),
        (((0,), (0,)), ((), ())),
        precision=lax.Precision.HIGHEST,
        preferred_element_type=jnp.float32,
    )
    inv = 1.0 / jnp.sqrt(total * scale + 1e-06)
    copies = []
    for chunk in range(chunks):
        size = tokens // chunks
        rows = pl.ds(chunk * size, size)
        part = inv[chunk * size:(chunk + 1) * size]
        for g in range(width // LANES):
            cols = pl.ds(g * LANES, LANES)
            out_ref[rows, cols] = (gated_ref[rows, cols].astype(jnp.float32) * part).astype(jnp.bfloat16)
        copies.append(pltpu.make_async_copy(out_ref.at[rows, :], out_hbm.at[rows, :], sems.at[chunk]))
        copies[-1].start()
    for copy in copies:
        copy.wait()


def per_device(hyena_q, hyena_k, hyena_v, filter_rate, filter_residue, skip_gain):
    n_ctx = lax.axis_size("ctx")
    n_tp = lax.axis_size("tp")
    tokens, width = hyena_q.shape
    groups = width // LANES
    f32, bf16 = jnp.float32, jnp.bfloat16
    rows = ORDER * groups
    half = rows // CORES
    shape = jax.ShapeDtypeStruct
    state = shape((rows, LANES), f32)
    table = shape((tokens * groups, LANES), f32)
    small = pltpu.VMEM((rows, LANES), f32)
    tile = pltpu.VMEM((tokens, width), bf16)
    n_x = n_ctx // (CORES * RINGS)
    pairs = [[CORES * i + c for c in range(CORES)] for i in range(n_ctx // CORES)]
    along_z = [
        [(x * RINGS + z) * CORES + c for z in range(RINGS)] for x in range(n_x) for c in range(CORES)
    ]
    along_x = [
        [(x * RINGS + z) * CORES + c for x in range(n_x) for c in range(CORES)] for z in range(RINGS)
    ]

    def swap(array, places):
        return lax.all_to_all(
            array, "ctx", split_axis=0, concat_axis=0, tiled=True, axis_index_groups=places
        )

    rate = filter_rate.T
    weights = shape((rows * SUBS, LANES), f32)
    modes = pltpu.VMEM((ORDER, width), f32)
    ends, z, e, q8, rate_rows = call(
        state_kernel, (state, table, weights, state, state),
        (tile, tile, modes, modes, pltpu.VMEM((groups, LANES), f32), pltpu.VMEM(table.shape, f32), small, small,
         pltpu.SemaphoreType.DMA((2, CHUNKS)), pltpu.SemaphoreType.DMA((3,))),
        "states", (pltpu.HBM,) * 5,
    )(*(
        pltpu.with_memory_space_constraint(array, pltpu.HBM)
        for array in (hyena_k, hyena_v, rate, filter_residue.T, skip_gain.reshape(groups, LANES))
    ))
    ends = lax.all_gather(ends, "ctx", axis_index_groups=pairs)
    totals = call(chip_kernel, shape((RINGS, half, LANES), Z_TYPE), (), "chip")(rate_rows, ends)
    totals = swap(totals, along_z)
    wholes = call(ring_kernel, shape((n_x * CORES, half, LANES), X_TYPE), (), "ring")(rate_rows, totals)
    wholes = swap(wholes, along_x)
    gated, sums = call(
        gate_kernel,
        (shape((tokens, width), bf16), shape((n_tp, tokens), f32)),
        (pltpu.VMEM((tokens, LANES), f32), small), "gate",
    )(hyena_q, z, e, q8, rate_rows, wholes, ends)
    all_sums = lax.all_to_all(sums, "tp", split_axis=0, concat_axis=0, tiled=True)
    return call(
        functools.partial(norm_kernel, 1.0 / (n_tp * width)),
        shape((tokens, width), bf16), (tile, pltpu.SemaphoreType.DMA((4,))), "norm",
        (pltpu.VMEM,) * 2, pltpu.HBM,
    )(all_sums, gated)


def solution(mesh):
    in_specs = (
        P("ctx", "tp"),
        P("ctx", "tp"),
        P("ctx", "tp"),
        P("tp", None),
        P("tp", None),
        P("tp"),
    )
    return jax.shard_map(
        per_device, mesh=mesh, in_specs=in_specs, out_specs=P("ctx", "tp"), check_vma=False
    )
```

```python
import functools

import jax
import jax.numpy as jnp
from jax import lax
from jax.experimental import pallas as pl
from jax.experimental.pallas import tpu as pltpu
from jax.sharding import PartitionSpec as P

ORDER = 16
LANES = 128
SUBS = 8
CORES = 2
RINGS = 8
RING_ORDER = (5, 6, 7, 0, 1, 2, 3, 4)
TP_ORDER = [4, 5, 6, 7, 0, 1, 2, 3]
X_ORDER = ((2, 1), (0, 0), (0, 1), (1, 0), (1, 1), (2, 0), (3, 0), (3, 1))
CHUNKS = 2
Z_TYPE = jnp.bfloat16
X_TYPE = jnp.bfloat16


def call(kernel, out_shape, scratch=(), name=None, ins=None, outs=None):
    specs = {}
    if ins is not None:
        specs["in_specs"] = [pl.BlockSpec(memory_space=space) for space in ins]
    if outs is not None:
        specs["out_specs"] = pl.BlockSpec(memory_space=outs)
    return pl.pallas_call(
        kernel,
        out_shape=out_shape,
        scratch_shapes=scratch,
        name=name,
        compiler_params=pltpu.CompilerParams(vmem_limit_bytes=48 * 1024 * 1024),
        **specs,
    )


def fill_modes(src_ref, dst_ref, fn):
    groups = src_ref.shape[1] // LANES
    for g in range(groups):
        dst_ref[pl.ds(g, ORDER, stride=groups), :] = fn(src_ref[:, pl.ds(g * LANES, LANES)])


def state_kernel(
    k_hbm, v_hbm, rate_hbm, res_hbm, skip_hbm, end_ref, z_ref, e_ref, q8_ref, rate_rows_ref,
    k_ref, v_ref, rate_ref, res_ref, skip_ref, u_ref, q_ref, r_ref, sems, mode_sems,
):
    tokens, width = k_ref.shape
    groups = width // LANES
    chunks = sems.shape[1]
    size = tokens // chunks

    def fetch(chunk):
        rows = pl.ds(chunk * size, size)
        return (
            pltpu.make_async_copy(k_hbm.at[rows, :], k_ref.at[rows, :], sems.at[0, chunk]),
            pltpu.make_async_copy(v_hbm.at[rows, :], v_ref.at[rows, :], sems.at[1, chunk]),
        )

    modes = (
        pltpu.make_async_copy(rate_hbm, rate_ref, mode_sems.at[0]),
        pltpu.make_async_copy(res_hbm, res_ref, mode_sems.at[1]),
        pltpu.make_async_copy(skip_hbm, skip_ref, mode_sems.at[2]),
    )
    for copy in modes:
        copy.start()
    for chunk in range(chunks):
        for copy in fetch(chunk):
            copy.start()
    for copy in modes:
        copy.wait()
    fill_modes(rate_ref, rate_rows_ref, lambda r: r)
    fill_modes(res_ref, r_ref, lambda r: r)
    q_ref[...] = jnp.exp(-rate_rows_ref[...])
    for m in range(ORDER):
        rows = pl.ds(m * groups, groups)
        q = q_ref[rows, :]
        w = r_ref[rows, :] * q
        for i in range(SUBS):
            e_ref[pl.ds(m * groups * SUBS + i, groups, stride=SUBS), :] = w
            w = w * q
        q2 = q * q
        q4 = q2 * q2
        q8_ref[rows, :] = q4 * q4
    rs = tuple(r_ref[pl.ds(m * groups, groups), :] for m in range(ORDER))
    qs = tuple(q_ref[pl.ds(m * groups, groups), :] for m in range(ORDER))
    xs = (jnp.zeros((SUBS, LANES), jnp.float32),) * ORDER
    for chunk in range(chunks):
        for copy in fetch(chunk):
            copy.wait()
        for pair in range(chunk * size // 16, (chunk + 1) * size // 16):
            rows = pl.ds(pair * 16, 16)
            for g in range(groups):
                cols = pl.ds(g * LANES, LANES)
                p = k_ref[rows, cols].astype(jnp.float32) * v_ref[rows, cols].astype(jnp.float32)
                p = p.astype(jnp.bfloat16).astype(jnp.float32)
                u_ref[pl.ds((2 * pair * groups + g) * SUBS, SUBS), :] = p[:SUBS]
                u_ref[pl.ds(((2 * pair + 1) * groups + g) * SUBS, SUBS), :] = p[SUBS:]

        def step(tb, xs):
            for i in range(SUBS):
                at = pl.ds(tb * groups * SUBS + i, groups, stride=SUBS)
                u = u_ref[at, :]
                terms, new = [skip_ref[...] * u], []
                for m in range(ORDER):
                    rows = pl.ds(m * groups, groups)
                    x = qs[m] * xs[m] + u
                    terms.append(rs[m] * x)
                    new.append(x)
                xs = tuple(new)
                while len(terms) > 1:
                    terms = [functools.reduce(jnp.add, terms[n:n + 2]) for n in range(0, len(terms), 2)]
                z_ref[at, :] = terms[0]
            return xs

        xs = lax.fori_loop(chunk * size // SUBS, (chunk + 1) * size // SUBS, step, xs)
    for m in range(ORDER):
        end_ref[pl.ds(m * groups, groups), :] = xs[m]


def decay_of(rate, positions):
    return jnp.exp(rate * -positions)


def half_rates(rate_ref):
    half = rate_ref.shape[0] // CORES
    core = lax.axis_index("ctx") % CORES
    return pl.ds(pl.multiple_of(core * half, SUBS), half)


def chip_kernel(rate_ref, ends_ref, total_ref):
    rows = half_rates(rate_ref)
    decay = decay_of(rate_ref[rows, :], float(LANES))
    total = (decay * ends_ref[0, rows, :] + ends_ref[1, rows, :]).astype(total_ref.dtype)
    for copy in range(total_ref.shape[0]):
        total_ref[copy] = total


def prefix(part, count, decay, place):
    run = jnp.zeros(decay.shape, jnp.float32)
    before = run
    for n in range(count):
        before = jnp.where(place == n, run, before)
        run = decay * run + part(n).astype(jnp.float32)
    return before, run


def ring_kernel(rate_ref, totals_ref, wholes_ref):
    me = lax.axis_index("ctx")
    decay = decay_of(rate_ref[half_rates(rate_ref), :], float(CORES * LANES))
    before, run = prefix(lambda n: totals_ref[RING_ORDER.index(n)], RINGS, decay, me // CORES % RINGS)
    x = me // (CORES * RINGS)
    for n in range(wholes_ref.shape[0]):
        wholes_ref[n] = jnp.where(x == X_ORDER[n][0], before, run).astype(wholes_ref.dtype)


def block_start(rate_ref, wholes_ref, ends_ref, s_ref):
    me = lax.axis_index("ctx")
    x, z, core = me // (CORES * RINGS), me // CORES % RINGS, me % CORES
    half = wholes_ref.shape[1]
    for h in range(CORES):
        rows = pl.ds(h * half, half)
        rate = rate_ref[rows, :]
        far, _ = prefix(
            lambda n: wholes_ref[X_ORDER.index((n, h))], wholes_ref.shape[0] // CORES,
            decay_of(rate, float(RINGS * CORES * LANES)), x,
        )
        near = wholes_ref[X_ORDER.index((0, h))]
        for n in range(1, wholes_ref.shape[0] // CORES):
            near = jnp.where(x == n, wholes_ref[X_ORDER.index((n, h))], near)
        near = near.astype(jnp.float32)
        first = decay_of(rate, float(CORES * LANES) * z.astype(jnp.float32)) * far + near
        second = decay_of(rate, float(LANES)) * first + ends_ref[0, rows, :]
        s_ref[rows, :] = jnp.where(core == 0, first, second)


def gate_kernel(q_ref, z_ref, e_ref, q8_ref, rate_ref, wholes_ref, ends_ref, gated_ref, sums_ref, sq_ref, s_ref):
    block_start(rate_ref, wholes_ref, ends_ref, s_ref)
    tokens, width = q_ref.shape
    groups = width // LANES
    for g in range(groups):
        vs, decays = [], []
        for m in range(ORDER):
            row = pl.ds(m * groups + g, 1)
            s = jnp.broadcast_to(s_ref[row, :], (SUBS, LANES))
            vs.append(s * e_ref[pl.ds((m * groups + g) * SUBS, SUBS), :])
            decays.append(jnp.broadcast_to(q8_ref[row, :], (SUBS, LANES)))
        for pair in range(tokens // 16):
            parts = []
            for half in range(2):
                tb = 2 * pair + half
                parts.append(z_ref[pl.ds((tb * groups + g) * SUBS, SUBS), :] + functools.reduce(jnp.add, vs))
                vs = [v * d for v, d in zip(vs, decays)]
            rows, cols = pl.ds(pair * 16, 16), pl.ds(g * LANES, LANES)
            wide = q_ref[rows, cols].astype(jnp.float32) * jnp.concatenate(parts, axis=0)
            gated = wide.astype(jnp.bfloat16)
            gated_ref[rows, cols] = gated
            square = gated.astype(jnp.float32)
            square = square * square
            if g == 0:
                sq_ref[rows, :] = square
            else:
                sq_ref[rows, :] = sq_ref[rows, :] + square
    sums = jnp.sum(sq_ref[...].T, axis=0, keepdims=True)
    sums_ref[...] = jnp.broadcast_to(sums, sums_ref.shape)


def norm_kernel(scale, sums_ref, gated_ref, out_hbm, out_ref, sems):
    tokens, width = gated_ref.shape
    chunks = sems.shape[0]
    total = jnp.sum(sums_ref[...], axis=0, keepdims=True)
    inv = 1.0 / jnp.sqrt(total * scale + 1e-06)
    inv = jnp.broadcast_to(inv, (LANES, tokens)).T
    copies = []
    for chunk in range(chunks):
        size = tokens // chunks
        rows = pl.ds(chunk * size, size)
        part = inv[chunk * size:(chunk + 1) * size]
        for g in range(width // LANES):
            cols = pl.ds(g * LANES, LANES)
            out_ref[rows, cols] = (gated_ref[rows, cols].astype(jnp.float32) * part).astype(jnp.bfloat16)
        copies.append(pltpu.make_async_copy(out_ref.at[rows, :], out_hbm.at[rows, :], sems.at[chunk]))
        copies[-1].start()
    for copy in copies:
        copy.wait()


def per_device(hyena_q, hyena_k, hyena_v, filter_rate, filter_residue, skip_gain):
    n_ctx = lax.axis_size("ctx")
    n_tp = lax.axis_size("tp")
    tokens, width = hyena_q.shape
    groups = width // LANES
    f32, bf16 = jnp.float32, jnp.bfloat16
    rows = ORDER * groups
    half = rows // CORES
    shape = jax.ShapeDtypeStruct
    state = shape((rows, LANES), f32)
    table = shape((tokens * groups, LANES), f32)
    small = pltpu.VMEM((rows, LANES), f32)
    tile = pltpu.VMEM((tokens, width), bf16)
    n_x = n_ctx // (CORES * RINGS)
    pairs = [[CORES * i + c for c in range(CORES)] for i in range(n_ctx // CORES)]
    along_z = [
        [(x * RINGS + z) * CORES + c for z in RING_ORDER] for x in range(n_x) for c in range(CORES)
    ]
    along_x = [
        [(x * RINGS + z) * CORES + c for x, c in X_ORDER] for z in range(RINGS)
    ]

    def swap(array, places):
        return lax.all_to_all(
            array, "ctx", split_axis=0, concat_axis=0, tiled=True, axis_index_groups=places
        )

    rate = filter_rate.T
    weights = shape((rows * SUBS, LANES), f32)
    modes = pltpu.VMEM((ORDER, width), f32)
    ends, z, e, q8, rate_rows = call(
        state_kernel, (state, table, weights, state, state),
        (tile, tile, modes, modes, pltpu.VMEM((groups, LANES), f32), pltpu.VMEM(table.shape, f32), small, small,
         pltpu.SemaphoreType.DMA((2, CHUNKS)), pltpu.SemaphoreType.DMA((3,))),
        "states", (pltpu.HBM,) * 5,
    )(*(
        pltpu.with_memory_space_constraint(array, pltpu.HBM)
        for array in (hyena_k, hyena_v, rate, filter_residue.T, skip_gain.reshape(groups, LANES))
    ))
    ends = lax.all_gather(ends, "ctx", axis_index_groups=pairs)
    totals = call(chip_kernel, shape((RINGS, half, LANES), Z_TYPE), (), "chip")(rate_rows, ends)
    totals = swap(totals, along_z)
    wholes = call(ring_kernel, shape((n_x * CORES, half, LANES), X_TYPE), (), "ring")(rate_rows, totals)
    wholes = swap(wholes, along_x)
    gated, sums = call(
        gate_kernel,
        (shape((tokens, width), bf16), shape((n_tp, tokens), f32)),
        (pltpu.VMEM((tokens, LANES), f32), small), "gate",
    )(hyena_q, z, e, q8, rate_rows, wholes, ends)
    all_sums = lax.all_to_all(
        sums, "tp", split_axis=0, concat_axis=0, tiled=True, axis_index_groups=[TP_ORDER]
    )
    return call(
        functools.partial(norm_kernel, 1.0 / (n_tp * width)),
        shape((tokens, width), bf16), (tile, pltpu.SemaphoreType.DMA((4,))), "norm",
        (pltpu.VMEM,) * 2, pltpu.HBM,
    )(all_sums, gated)


def solution(mesh):
    in_specs = (
        P("ctx", "tp"),
        P("ctx", "tp"),
        P("ctx", "tp"),
        P("tp", None),
        P("tp", None),
        P("tp"),
    )
    return jax.shard_map(
        per_device, mesh=mesh, in_specs=in_specs, out_specs=P("ctx", "tp"), check_vma=False
    )
```

```python
import functools

import jax
import jax.numpy as jnp
from jax import lax
from jax.experimental import pallas as pl
from jax.experimental.pallas import tpu as pltpu
from jax.sharding import PartitionSpec as P

ORDER = 16
LANES = 128
SUBS = 8
CORES = 2
RINGS = 8
RING_ORDER = (6, 7, 0, 1, 2, 3, 4, 5)
TP_ORDER = [4, 5, 6, 7, 0, 1, 2, 3]
X_ORDER = ((2, 1), (0, 0), (0, 1), (1, 0), (1, 1), (2, 0), (3, 0), (3, 1))
CHUNKS = 2
Z_TYPE = jnp.bfloat16
X_TYPE = jnp.bfloat16


def call(kernel, out_shape, scratch=(), name=None, ins=None, outs=None, aliases={}):
    specs = {}
    if ins is not None:
        specs["in_specs"] = [pl.BlockSpec(memory_space=space) for space in ins]
    if outs is not None:
        specs["out_specs"] = pl.BlockSpec(memory_space=outs)
    return pl.pallas_call(
        kernel,
        out_shape=out_shape,
        scratch_shapes=scratch,
        input_output_aliases=aliases,
        name=name,
        compiler_params=pltpu.CompilerParams(vmem_limit_bytes=48 * 1024 * 1024),
        **specs,
    )


def fill_modes(src_ref, dst_ref, fn):
    groups = src_ref.shape[1] // LANES
    for g in range(groups):
        dst_ref[pl.ds(g, ORDER, stride=groups), :] = fn(src_ref[:, pl.ds(g * LANES, LANES)])


def state_kernel(
    k_hbm, v_hbm, rate_hbm, res_hbm, skip_hbm, end_ref, z_ref, e_ref, q8_ref, rate_rows_ref, u_ref, r_ref, skip_ref,
    k_ref, v_ref, rate_ref, res_ref, q_ref, sems, mode_sems,
):
    tokens, width = k_ref.shape
    groups = width // LANES
    chunks = sems.shape[1]
    size = tokens // chunks

    def fetch(chunk):
        rows = pl.ds(chunk * size, size)
        return (
            pltpu.make_async_copy(k_hbm.at[rows, :], k_ref.at[rows, :], sems.at[0, chunk]),
            pltpu.make_async_copy(v_hbm.at[rows, :], v_ref.at[rows, :], sems.at[1, chunk]),
        )

    modes = (
        pltpu.make_async_copy(rate_hbm, rate_ref, mode_sems.at[0]),
        pltpu.make_async_copy(res_hbm, res_ref, mode_sems.at[1]),
        pltpu.make_async_copy(skip_hbm, skip_ref, mode_sems.at[2]),
    )
    for copy in modes:
        copy.start()
    for chunk in range(chunks):
        for copy in fetch(chunk):
            copy.start()
    for copy in modes:
        copy.wait()
    fill_modes(rate_ref, rate_rows_ref, lambda r: r)
    fill_modes(res_ref, r_ref, lambda r: r)
    q_ref[...] = jnp.exp(-rate_rows_ref[...])
    for m in range(ORDER):
        rows = pl.ds(m * groups, groups)
        q = q_ref[rows, :]
        w = r_ref[rows, :] * q
        for i in range(SUBS):
            e_ref[pl.ds(m * groups * SUBS + i, groups, stride=SUBS), :] = w
            w = w * q
        q2 = q * q
        q4 = q2 * q2
        q8_ref[rows, :] = q4 * q4
    for chunk in range(chunks):
        for copy in fetch(chunk):
            copy.wait()
        for pair in range(chunk * size // 16, (chunk + 1) * size // 16):
            rows = pl.ds(pair * 16, 16)
            for g in range(groups):
                cols = pl.ds(g * LANES, LANES)
                p = k_ref[rows, cols].astype(jnp.float32) * v_ref[rows, cols].astype(jnp.float32)
                p = p.astype(jnp.bfloat16).astype(jnp.float32)
                u_ref[pl.ds((2 * pair * groups + g) * SUBS, SUBS), :] = p[:SUBS]
                u_ref[pl.ds(((2 * pair + 1) * groups + g) * SUBS, SUBS), :] = p[SUBS:]
        blocks = (chunk * size // SUBS, (chunk + 1) * size // SUBS)

        @pl.when(defers())
        def _():
            recur(*blocks, end_ref, u_ref, q_ref, None, None, None)

        @pl.when(jnp.logical_not(defers()))
        def _():
            recur(*blocks, end_ref, u_ref, q_ref, r_ref, skip_ref, z_ref)


def defers():
    return lax.axis_index("ctx") // CORES % RINGS >= RINGS // 2


def recur(first, last, x_ref, u_ref, q_ref, r_ref, skip_ref, z_ref):
    groups = SUBS
    rows = [pl.ds(m * groups, groups) for m in range(ORDER)]
    qs = tuple(q_ref[at, :] for at in rows)
    if z_ref is not None:
        rs = tuple(r_ref[at, :] for at in rows)

    def step(tb, xs):
        for i in range(SUBS):
            at = pl.ds(tb * groups * SUBS + i, groups, stride=SUBS)
            u = u_ref[at, :]
            xs = tuple(q * x + u for q, x in zip(qs, xs))
            if z_ref is not None:
                terms = [skip_ref[...] * u] + [r * x for r, x in zip(rs, xs)]
                while len(terms) > 1:
                    terms = [functools.reduce(jnp.add, terms[n:n + 2]) for n in range(0, len(terms), 2)]
                z_ref[at, :] = terms[0]
        return xs

    if first == 0:
        xs = (jnp.zeros((groups, LANES), jnp.float32),) * ORDER
    else:
        xs = tuple(x_ref[at, :] for at in rows)
    xs = lax.fori_loop(first, last, step, xs)
    for at, x in zip(rows, xs):
        x_ref[at, :] = x


def decay_of(rate, positions):
    return jnp.exp(rate * -positions)


def half_rates(rate_ref):
    half = rate_ref.shape[0] // CORES
    core = lax.axis_index("ctx") % CORES
    return pl.ds(pl.multiple_of(core * half, SUBS), half)


def chip_kernel(rate_ref, ends_ref, total_ref):
    rows = half_rates(rate_ref)
    decay = decay_of(rate_ref[rows, :], float(LANES))
    total = (decay * ends_ref[0, rows, :] + ends_ref[1, rows, :]).astype(total_ref.dtype)
    for copy in range(total_ref.shape[0]):
        total_ref[copy] = total


def prefix(part, count, decay, place):
    run = jnp.zeros(decay.shape, jnp.float32)
    before = run
    for n in range(count):
        before = jnp.where(place == n, run, before)
        run = decay * run + part(n).astype(jnp.float32)
    return before, run


def ring_kernel(rate_ref, totals_ref, u_ref, r_ref, skip_ref, z_in_ref, wholes_ref, z_ref, q_ref, x_ref):
    me = lax.axis_index("ctx")
    decay = decay_of(rate_ref[half_rates(rate_ref), :], float(CORES * LANES))
    before, run = prefix(lambda n: totals_ref[RING_ORDER.index(n)], RINGS, decay, me // CORES % RINGS)
    x = me // (CORES * RINGS)
    for n in range(wholes_ref.shape[0]):
        wholes_ref[n] = jnp.where(x == X_ORDER[n][0], before, run).astype(wholes_ref.dtype)

    @pl.when(defers())
    def _():
        q_ref[...] = jnp.exp(-rate_ref[...])
        recur(0, u_ref.shape[0] // (SUBS * SUBS), x_ref, u_ref, q_ref, r_ref, skip_ref, z_ref)


def block_start(rate_ref, wholes_ref, ends_ref, s_ref):
    me = lax.axis_index("ctx")
    x, z, core = me // (CORES * RINGS), me // CORES % RINGS, me % CORES
    half = wholes_ref.shape[1]
    for h in range(CORES):
        rows = pl.ds(h * half, half)
        rate = rate_ref[rows, :]
        far, _ = prefix(
            lambda n: wholes_ref[X_ORDER.index((n, h))], wholes_ref.shape[0] // CORES,
            decay_of(rate, float(RINGS * CORES * LANES)), x,
        )
        near = wholes_ref[X_ORDER.index((0, h))]
        for n in range(1, wholes_ref.shape[0] // CORES):
            near = jnp.where(x == n, wholes_ref[X_ORDER.index((n, h))], near)
        near = near.astype(jnp.float32)
        first = decay_of(rate, float(CORES * LANES) * z.astype(jnp.float32)) * far + near
        second = decay_of(rate, float(LANES)) * first + ends_ref[0, rows, :]
        s_ref[rows, :] = jnp.where(core == 0, first, second)


def gate_kernel(q_ref, z_ref, e_ref, q8_ref, rate_ref, wholes_ref, ends_ref, gated_ref, sums_ref, sq_ref, s_ref):
    block_start(rate_ref, wholes_ref, ends_ref, s_ref)
    tokens, width = q_ref.shape
    groups = width // LANES
    for g in range(groups):
        vs, decays = [], []
        for m in range(ORDER):
            row = pl.ds(m * groups + g, 1)
            s = jnp.broadcast_to(s_ref[row, :], (SUBS, LANES))
            vs.append(s * e_ref[pl.ds((m * groups + g) * SUBS, SUBS), :])
            decays.append(jnp.broadcast_to(q8_ref[row, :], (SUBS, LANES)))
        for pair in range(tokens // 16):
            parts = []
            for half in range(2):
                tb = 2 * pair + half
                parts.append(z_ref[pl.ds((tb * groups + g) * SUBS, SUBS), :] + functools.reduce(jnp.add, vs))
                vs = [v * d for v, d in zip(vs, decays)]
            rows, cols = pl.ds(pair * 16, 16), pl.ds(g * LANES, LANES)
            wide = q_ref[rows, cols].astype(jnp.float32) * jnp.concatenate(parts, axis=0)
            gated = wide.astype(jnp.bfloat16)
            gated_ref[rows, cols] = gated
            square = gated.astype(jnp.float32)
            square = square * square
            if g == 0:
                sq_ref[rows, :] = square
            else:
                sq_ref[rows, :] = sq_ref[rows, :] + square
    sums = jnp.sum(sq_ref[...].T, axis=0, keepdims=True)
    sums_ref[...] = jnp.broadcast_to(sums, sums_ref.shape)


def norm_kernel(scale, sums_ref, gated_ref, out_hbm, out_ref, sems):
    tokens, width = gated_ref.shape
    chunks = sems.shape[0]
    total = jnp.sum(sums_ref[...], axis=0, keepdims=True)
    inv = 1.0 / jnp.sqrt(total * scale + 1e-06)
    inv = jnp.broadcast_to(inv, (LANES, tokens)).T
    copies = []
    for chunk in range(chunks):
        size = tokens // chunks
        rows = pl.ds(chunk * size, size)
        part = inv[chunk * size:(chunk + 1) * size]
        for g in range(width // LANES):
            cols = pl.ds(g * LANES, LANES)
            out_ref[rows, cols] = (gated_ref[rows, cols].astype(jnp.float32) * part).astype(jnp.bfloat16)
        copies.append(pltpu.make_async_copy(out_ref.at[rows, :], out_hbm.at[rows, :], sems.at[chunk]))
        copies[-1].start()
    for copy in copies:
        copy.wait()


def per_device(hyena_q, hyena_k, hyena_v, filter_rate, filter_residue, skip_gain):
    n_ctx = lax.axis_size("ctx")
    n_tp = lax.axis_size("tp")
    tokens, width = hyena_q.shape
    groups = width // LANES
    f32, bf16 = jnp.float32, jnp.bfloat16
    rows = ORDER * groups
    half = rows // CORES
    shape = jax.ShapeDtypeStruct
    state = shape((rows, LANES), f32)
    table = shape((tokens * groups, LANES), f32)
    small = pltpu.VMEM((rows, LANES), f32)
    tile = pltpu.VMEM((tokens, width), bf16)
    n_x = n_ctx // (CORES * RINGS)
    pairs = [[CORES * i + c for c in range(CORES)] for i in range(n_ctx // CORES)]
    along_z = [
        [(x * RINGS + z) * CORES + c for z in RING_ORDER] for x in range(n_x) for c in range(CORES)
    ]
    along_x = [
        [(x * RINGS + z) * CORES + c for x, c in X_ORDER] for z in range(RINGS)
    ]

    def swap(array, places):
        return lax.all_to_all(
            array, "ctx", split_axis=0, concat_axis=0, tiled=True, axis_index_groups=places
        )

    rate = filter_rate.T
    weights = shape((rows * SUBS, LANES), f32)
    modes = pltpu.VMEM((ORDER, width), f32)
    ends, z, e, q8, rate_rows, u, residues, skip = call(
        state_kernel, (state, table, weights, state, state, table, state, shape((groups, LANES), f32)),
        (tile, tile, modes, modes, small,
         pltpu.SemaphoreType.DMA((2, CHUNKS)), pltpu.SemaphoreType.DMA((3,))),
        "states", (pltpu.HBM,) * 5,
    )(*(
        pltpu.with_memory_space_constraint(array, pltpu.HBM)
        for array in (hyena_k, hyena_v, rate, filter_residue.T, skip_gain.reshape(groups, LANES))
    ))
    ends = lax.all_gather(ends, "ctx", axis_index_groups=pairs)
    totals = call(chip_kernel, shape((RINGS, half, LANES), Z_TYPE), (), "chip")(rate_rows, ends)
    totals = swap(totals, along_z)
    wholes, z = call(
        ring_kernel, (shape((n_x * CORES, half, LANES), X_TYPE), table), (small, small), "ring", aliases={5: 1},
    )(rate_rows, totals, u, residues, skip, z)
    wholes = swap(wholes, along_x)
    gated, sums = call(
        gate_kernel,
        (shape((tokens, width), bf16), shape((n_tp, tokens), f32)),
        (pltpu.VMEM((tokens, LANES), f32), small), "gate",
    )(hyena_q, z, e, q8, rate_rows, wholes, ends)
    all_sums = lax.all_to_all(
        sums, "tp", split_axis=0, concat_axis=0, tiled=True, axis_index_groups=[TP_ORDER]
    )
    return call(
        functools.partial(norm_kernel, 1.0 / (n_tp * width)),
        shape((tokens, width), bf16), (tile, pltpu.SemaphoreType.DMA((4,))), "norm",
        (pltpu.VMEM,) * 2, pltpu.HBM,
    )(all_sums, gated)


def solution(mesh):
    in_specs = (
        P("ctx", "tp"),
        P("ctx", "tp"),
        P("ctx", "tp"),
        P("tp", None),
        P("tp", None),
        P("tp"),
    )
    return jax.shard_map(
        per_device, mesh=mesh, in_specs=in_specs, out_specs=P("ctx", "tp"), check_vma=False
    )
```

```python
import functools

import jax
import jax.numpy as jnp
from jax import lax
from jax.experimental import pallas as pl
from jax.experimental.pallas import tpu as pltpu
from jax.sharding import PartitionSpec as P

ORDER = 16
LANES = 128
SUBS = 8
CORES = 2
RINGS = 8
RING_ORDER = (6, 7, 0, 1, 2, 3, 4, 5)
TP_ORDER = [4, 5, 6, 7, 0, 1, 2, 3]
X_ORDER = ((2, 1), (0, 0), (0, 1), (1, 0), (1, 1), (2, 0), (3, 0), (3, 1))
CHUNKS = 2
Z_TYPE = jnp.bfloat16
X_TYPE = jnp.bfloat16


def call(kernel, out_shape, scratch=(), name=None, ins=None, outs=None, aliases={}):
    specs = {}
    if ins is not None:
        specs["in_specs"] = [pl.BlockSpec(memory_space=space) for space in ins]
    if outs is not None:
        specs["out_specs"] = pl.BlockSpec(memory_space=outs)
    return pl.pallas_call(
        kernel,
        out_shape=out_shape,
        scratch_shapes=scratch,
        input_output_aliases=aliases,
        name=name,
        compiler_params=pltpu.CompilerParams(vmem_limit_bytes=48 * 1024 * 1024),
        **specs,
    )


def fill_modes(src_ref, dst_ref, fn):
    groups = src_ref.shape[1] // LANES
    for g in range(groups):
        dst_ref[pl.ds(g, ORDER, stride=groups), :] = fn(src_ref[:, pl.ds(g * LANES, LANES)])


def tables(q_ref, r_ref, e_ref, q8_ref):
    groups = SUBS
    for m in range(ORDER):
        rows = pl.ds(m * groups, groups)
        q = q_ref[rows, :]
        w = r_ref[rows, :] * q
        for i in range(SUBS):
            e_ref[pl.ds(m * groups * SUBS + i, groups, stride=SUBS), :] = w
            w = w * q
        q2 = q * q
        q4 = q2 * q2
        q8_ref[rows, :] = q4 * q4


def state_kernel(
    k_hbm, v_hbm, rate_hbm, res_hbm, skip_hbm, end_ref, z_ref, e_ref, q8_ref, rate_rows_ref, u_ref, r_ref, skip_ref,
    k_ref, v_ref, rate_ref, res_ref, q_ref, sems, mode_sems,
):
    tokens, width = k_ref.shape
    groups = width // LANES
    chunks = sems.shape[1]
    size = tokens // chunks

    def fetch(chunk):
        rows = pl.ds(chunk * size, size)
        return (
            pltpu.make_async_copy(k_hbm.at[rows, :], k_ref.at[rows, :], sems.at[0, chunk]),
            pltpu.make_async_copy(v_hbm.at[rows, :], v_ref.at[rows, :], sems.at[1, chunk]),
        )

    modes = (
        pltpu.make_async_copy(rate_hbm, rate_ref, mode_sems.at[0]),
        pltpu.make_async_copy(res_hbm, res_ref, mode_sems.at[1]),
        pltpu.make_async_copy(skip_hbm, skip_ref, mode_sems.at[2]),
    )
    for copy in modes:
        copy.start()
    for chunk in range(chunks):
        for copy in fetch(chunk):
            copy.start()
    for copy in modes:
        copy.wait()
    fill_modes(rate_ref, rate_rows_ref, lambda r: r)
    fill_modes(res_ref, r_ref, lambda r: r)
    q_ref[...] = jnp.exp(-rate_rows_ref[...])
    @pl.when(jnp.logical_not(defers()))
    def _():
        tables(q_ref, r_ref, e_ref, q8_ref)

    for chunk in range(chunks):
        for copy in fetch(chunk):
            copy.wait()
        for pair in range(chunk * size // 16, (chunk + 1) * size // 16):
            rows = pl.ds(pair * 16, 16)
            for g in range(groups):
                cols = pl.ds(g * LANES, LANES)
                p = k_ref[rows, cols].astype(jnp.float32) * v_ref[rows, cols].astype(jnp.float32)
                p = p.astype(jnp.bfloat16).astype(jnp.float32)
                u_ref[pl.ds((2 * pair * groups + g) * SUBS, SUBS), :] = p[:SUBS]
                u_ref[pl.ds(((2 * pair + 1) * groups + g) * SUBS, SUBS), :] = p[SUBS:]
        blocks = (chunk * size // SUBS, (chunk + 1) * size // SUBS)

        @pl.when(defers())
        def _():
            recur(*blocks, end_ref, u_ref, q_ref, None, None, None)

        @pl.when(jnp.logical_not(defers()))
        def _():
            recur(*blocks, end_ref, u_ref, q_ref, r_ref, skip_ref, z_ref)


def defers():
    return lax.axis_index("ctx") // CORES % RINGS >= RINGS // 2


def recur(first, last, x_ref, u_ref, q_ref, r_ref, skip_ref, z_ref):
    groups = SUBS
    rows = [pl.ds(m * groups, groups) for m in range(ORDER)]
    qs = tuple(q_ref[at, :] for at in rows)
    if z_ref is not None:
        rs = tuple(r_ref[at, :] for at in rows)

    def step(tb, xs):
        for i in range(SUBS):
            at = pl.ds(tb * groups * SUBS + i, groups, stride=SUBS)
            u = u_ref[at, :]
            xs = tuple(q * x + u for q, x in zip(qs, xs))
            if z_ref is not None:
                terms = [skip_ref[...] * u] + [r * x for r, x in zip(rs, xs)]
                while len(terms) > 1:
                    terms = [functools.reduce(jnp.add, terms[n:n + 2]) for n in range(0, len(terms), 2)]
                z_ref[at, :] = terms[0]
        return xs

    if first == 0:
        xs = (jnp.zeros((groups, LANES), jnp.float32),) * ORDER
    else:
        xs = tuple(x_ref[at, :] for at in rows)
    xs = lax.fori_loop(first, last, step, xs)
    for at, x in zip(rows, xs):
        x_ref[at, :] = x


def decay_of(rate, positions):
    return jnp.exp(rate * -positions)


def half_rates(rate_ref):
    half = rate_ref.shape[0] // CORES
    core = lax.axis_index("ctx") % CORES
    return pl.ds(pl.multiple_of(core * half, SUBS), half)


def chip_kernel(rate_ref, ends_ref, total_ref):
    rows = half_rates(rate_ref)
    decay = decay_of(rate_ref[rows, :], float(LANES))
    total = (decay * ends_ref[0, rows, :] + ends_ref[1, rows, :]).astype(total_ref.dtype)
    for copy in range(total_ref.shape[0]):
        total_ref[copy] = total


def prefix(part, count, decay, place):
    run = jnp.zeros(decay.shape, jnp.float32)
    before = run
    for n in range(count):
        before = jnp.where(place == n, run, before)
        run = decay * run + part(n).astype(jnp.float32)
    return before, run


def ring_kernel(rate_ref, totals_ref, u_ref, r_ref, skip_ref, z_in_ref, e_in_ref, q8_in_ref, wholes_ref, z_ref, e_ref, q8_ref, q_ref, x_ref):
    me = lax.axis_index("ctx")
    decay = decay_of(rate_ref[half_rates(rate_ref), :], float(CORES * LANES))
    before, run = prefix(lambda n: totals_ref[RING_ORDER.index(n)], RINGS, decay, me // CORES % RINGS)
    x = me // (CORES * RINGS)
    for n in range(wholes_ref.shape[0]):
        wholes_ref[n] = jnp.where(x == X_ORDER[n][0], before, run).astype(wholes_ref.dtype)

    @pl.when(defers())
    def _():
        q_ref[...] = jnp.exp(-rate_ref[...])
        tables(q_ref, r_ref, e_ref, q8_ref)
        recur(0, u_ref.shape[0] // (SUBS * SUBS), x_ref, u_ref, q_ref, r_ref, skip_ref, z_ref)


def block_start(rate_ref, wholes_ref, ends_ref, s_ref):
    me = lax.axis_index("ctx")
    x, z, core = me // (CORES * RINGS), me // CORES % RINGS, me % CORES
    half = wholes_ref.shape[1]
    for h in range(CORES):
        rows = pl.ds(h * half, half)
        rate = rate_ref[rows, :]
        far, _ = prefix(
            lambda n: wholes_ref[X_ORDER.index((n, h))], wholes_ref.shape[0] // CORES,
            decay_of(rate, float(RINGS * CORES * LANES)), x,
        )
        near = wholes_ref[X_ORDER.index((0, h))]
        for n in range(1, wholes_ref.shape[0] // CORES):
            near = jnp.where(x == n, wholes_ref[X_ORDER.index((n, h))], near)
        near = near.astype(jnp.float32)
        first = decay_of(rate, float(CORES * LANES) * z.astype(jnp.float32)) * far + near
        second = decay_of(rate, float(LANES)) * first + ends_ref[0, rows, :]
        s_ref[rows, :] = jnp.where(core == 0, first, second)


def gate_kernel(q_ref, z_ref, e_ref, q8_ref, rate_ref, wholes_ref, ends_ref, gated_ref, sums_ref, sq_ref, s_ref):
    block_start(rate_ref, wholes_ref, ends_ref, s_ref)
    tokens, width = q_ref.shape
    groups = width // LANES
    for g in range(groups):
        vs, decays = [], []
        for m in range(ORDER):
            row = pl.ds(m * groups + g, 1)
            s = jnp.broadcast_to(s_ref[row, :], (SUBS, LANES))
            vs.append(s * e_ref[pl.ds((m * groups + g) * SUBS, SUBS), :])
            decays.append(jnp.broadcast_to(q8_ref[row, :], (SUBS, LANES)))
        for pair in range(tokens // 16):
            parts = []
            for half in range(2):
                tb = 2 * pair + half
                parts.append(z_ref[pl.ds((tb * groups + g) * SUBS, SUBS), :] + functools.reduce(jnp.add, vs))
                vs = [v * d for v, d in zip(vs, decays)]
            rows, cols = pl.ds(pair * 16, 16), pl.ds(g * LANES, LANES)
            wide = q_ref[rows, cols].astype(jnp.float32) * jnp.concatenate(parts, axis=0)
            gated = wide.astype(jnp.bfloat16)
            gated_ref[rows, cols] = gated
            square = gated.astype(jnp.float32)
            square = square * square
            if g == 0:
                sq_ref[rows, :] = square
            else:
                sq_ref[rows, :] = sq_ref[rows, :] + square
    sums = jnp.sum(sq_ref[...].T, axis=0, keepdims=True)
    sums_ref[...] = jnp.broadcast_to(sums, sums_ref.shape)


def norm_kernel(scale, sums_ref, gated_ref, out_hbm, out_ref, sems):
    tokens, width = gated_ref.shape
    chunks = sems.shape[0]
    total = jnp.sum(sums_ref[...], axis=0, keepdims=True)
    inv = 1.0 / jnp.sqrt(total * scale + 1e-06)
    inv = jnp.broadcast_to(inv, (LANES, tokens)).T
    copies = []
    for chunk in range(chunks):
        size = tokens // chunks
        rows = pl.ds(chunk * size, size)
        part = inv[chunk * size:(chunk + 1) * size]
        for g in range(width // LANES):
            cols = pl.ds(g * LANES, LANES)
            out_ref[rows, cols] = (gated_ref[rows, cols].astype(jnp.float32) * part).astype(jnp.bfloat16)
        copies.append(pltpu.make_async_copy(out_ref.at[rows, :], out_hbm.at[rows, :], sems.at[chunk]))
        copies[-1].start()
    for copy in copies:
        copy.wait()


def per_device(hyena_q, hyena_k, hyena_v, filter_rate, filter_residue, skip_gain):
    n_ctx = lax.axis_size("ctx")
    n_tp = lax.axis_size("tp")
    tokens, width = hyena_q.shape
    groups = width // LANES
    f32, bf16 = jnp.float32, jnp.bfloat16
    rows = ORDER * groups
    half = rows // CORES
    shape = jax.ShapeDtypeStruct
    state = shape((rows, LANES), f32)
    table = shape((tokens * groups, LANES), f32)
    small = pltpu.VMEM((rows, LANES), f32)
    tile = pltpu.VMEM((tokens, width), bf16)
    n_x = n_ctx // (CORES * RINGS)
    pairs = [[CORES * i + c for c in range(CORES)] for i in range(n_ctx // CORES)]
    along_z = [
        [(x * RINGS + z) * CORES + c for z in RING_ORDER] for x in range(n_x) for c in range(CORES)
    ]
    along_x = [
        [(x * RINGS + z) * CORES + c for x, c in X_ORDER] for z in range(RINGS)
    ]

    def swap(array, places):
        return lax.all_to_all(
            array, "ctx", split_axis=0, concat_axis=0, tiled=True, axis_index_groups=places
        )

    rate = filter_rate.T
    weights = shape((rows * SUBS, LANES), f32)
    modes = pltpu.VMEM((ORDER, width), f32)
    ends, z, e, q8, rate_rows, u, residues, skip = call(
        state_kernel, (state, table, weights, state, state, table, state, shape((groups, LANES), f32)),
        (tile, tile, modes, modes, small,
         pltpu.SemaphoreType.DMA((2, CHUNKS)), pltpu.SemaphoreType.DMA((3,))),
        "states", (pltpu.HBM,) * 5,
    )(*(
        pltpu.with_memory_space_constraint(array, pltpu.HBM)
        for array in (hyena_k, hyena_v, rate, filter_residue.T, skip_gain.reshape(groups, LANES))
    ))
    ends = lax.all_gather(ends, "ctx", axis_index_groups=pairs)
    totals = call(chip_kernel, shape((RINGS, half, LANES), Z_TYPE), (), "chip")(rate_rows, ends)
    totals = swap(totals, along_z)
    wholes, z, e, q8 = call(
        ring_kernel, (shape((n_x * CORES, half, LANES), X_TYPE), table, weights, state), (small, small), "ring",
        aliases={5: 1, 6: 2, 7: 3},
    )(rate_rows, totals, u, residues, skip, z, e, q8)
    wholes = swap(wholes, along_x)
    gated, sums = call(
        gate_kernel,
        (shape((tokens, width), bf16), shape((n_tp, tokens), f32)),
        (pltpu.VMEM((tokens, LANES), f32), small), "gate",
    )(hyena_q, z, e, q8, rate_rows, wholes, ends)
    all_sums = lax.all_to_all(
        sums, "tp", split_axis=0, concat_axis=0, tiled=True, axis_index_groups=[TP_ORDER]
    )
    return call(
        functools.partial(norm_kernel, 1.0 / (n_tp * width)),
        shape((tokens, width), bf16), (tile, pltpu.SemaphoreType.DMA((4,))), "norm",
        (pltpu.VMEM,) * 2, pltpu.HBM,
    )(all_sums, gated)


def solution(mesh):
    in_specs = (
        P("ctx", "tp"),
        P("ctx", "tp"),
        P("ctx", "tp"),
        P("tp", None),
        P("tp", None),
        P("tp"),
    )
    return jax.shard_map(
        per_device, mesh=mesh, in_specs=in_specs, out_specs=P("ctx", "tp"), check_vma=False
    )
```

```python
import functools

import jax
import jax.numpy as jnp
from jax import lax
from jax.experimental import pallas as pl
from jax.experimental.pallas import tpu as pltpu
from jax.sharding import PartitionSpec as P

ORDER = 16
LANES = 128
SUBS = 8
CORES = 2
RINGS = 8
RING_ORDER = (6, 7, 0, 1, 2, 3, 4, 5)
TP_ORDER = [4, 5, 6, 7, 0, 1, 2, 3]
X_ORDER = ((2, 1), (0, 0), (0, 1), (1, 0), (1, 1), (2, 0), (3, 0), (3, 1))
CHUNKS = 2
Z_TYPE = jnp.bfloat16
X_TYPE = jnp.bfloat16


def call(kernel, out_shape, scratch=(), name=None, ins=None, outs=None, aliases={}):
    specs = {}
    if ins is not None:
        specs["in_specs"] = [pl.BlockSpec(memory_space=space) for space in ins]
    if outs is not None:
        specs["out_specs"] = pl.BlockSpec(memory_space=outs)
    return pl.pallas_call(
        kernel,
        out_shape=out_shape,
        scratch_shapes=scratch,
        input_output_aliases=aliases,
        name=name,
        compiler_params=pltpu.CompilerParams(vmem_limit_bytes=48 * 1024 * 1024),
        **specs,
    )


def fill_modes(src_ref, dst_ref, fn):
    groups = src_ref.shape[1] // LANES
    for g in range(groups):
        dst_ref[pl.ds(g, ORDER, stride=groups), :] = fn(src_ref[:, pl.ds(g * LANES, LANES)])


def tables(q_ref, r_ref, e_ref, q8_ref):
    groups = SUBS
    for m in range(ORDER):
        rows = pl.ds(m * groups, groups)
        q = q_ref[rows, :]
        w = r_ref[rows, :] * q
        for i in range(SUBS):
            e_ref[pl.ds(m * groups * SUBS + i, groups, stride=SUBS), :] = w
            w = w * q
        q2 = q * q
        q4 = q2 * q2
        q8_ref[rows, :] = q4 * q4


def state_kernel(
    k_hbm, v_hbm, rate_hbm, res_hbm, skip_hbm, end_ref, z_ref, e_ref, q8_ref, rate_rows_ref, u_ref, r_ref, skip_ref,
    k_ref, v_ref, rate_ref, res_ref, q_ref, sems, mode_sems,
):
    tokens, width = k_ref.shape
    groups = width // LANES
    chunks = sems.shape[1]
    size = tokens // chunks

    def fetch(chunk):
        rows = pl.ds(chunk * size, size)
        return (
            pltpu.make_async_copy(k_hbm.at[rows, :], k_ref.at[rows, :], sems.at[0, chunk]),
            pltpu.make_async_copy(v_hbm.at[rows, :], v_ref.at[rows, :], sems.at[1, chunk]),
        )

    modes = (
        pltpu.make_async_copy(rate_hbm, rate_ref, mode_sems.at[0]),
        pltpu.make_async_copy(res_hbm, res_ref, mode_sems.at[1]),
        pltpu.make_async_copy(skip_hbm, skip_ref, mode_sems.at[2]),
    )
    modes[0].start()
    for chunk in range(chunks):
        for copy in fetch(chunk):
            copy.start()
    for copy in modes[1:]:
        copy.start()
    modes[0].wait()
    fill_modes(rate_ref, rate_rows_ref, lambda r: r)
    q_ref[...] = jnp.exp(-rate_rows_ref[...])

    @pl.when(jnp.logical_not(defers()))
    def _():
        for copy in modes[1:]:
            copy.wait()
        fill_modes(res_ref, r_ref, lambda r: r)
        tables(q_ref, r_ref, e_ref, q8_ref)

    for chunk in range(chunks):
        for copy in fetch(chunk):
            copy.wait()
        for pair in range(chunk * size // 16, (chunk + 1) * size // 16):
            rows = pl.ds(pair * 16, 16)
            for g in range(groups):
                cols = pl.ds(g * LANES, LANES)
                p = k_ref[rows, cols].astype(jnp.float32) * v_ref[rows, cols].astype(jnp.float32)
                p = p.astype(jnp.bfloat16).astype(jnp.float32)
                u_ref[pl.ds((2 * pair * groups + g) * SUBS, SUBS), :] = p[:SUBS]
                u_ref[pl.ds(((2 * pair + 1) * groups + g) * SUBS, SUBS), :] = p[SUBS:]
        blocks = (chunk * size // SUBS, (chunk + 1) * size // SUBS)

        @pl.when(defers())
        def _():
            recur(*blocks, end_ref, u_ref, q_ref, None, None, None)

        @pl.when(jnp.logical_not(defers()))
        def _():
            recur(*blocks, end_ref, u_ref, q_ref, r_ref, skip_ref, z_ref)

    @pl.when(defers())
    def _():
        for copy in modes[1:]:
            copy.wait()
        fill_modes(res_ref, r_ref, lambda r: r)


def defers():
    return lax.axis_index("ctx") // CORES % RINGS >= RINGS // 2


def recur(first, last, x_ref, u_ref, q_ref, r_ref, skip_ref, z_ref):
    groups = SUBS
    rows = [pl.ds(m * groups, groups) for m in range(ORDER)]
    qs = tuple(q_ref[at, :] for at in rows)
    if z_ref is not None:
        rs = tuple(r_ref[at, :] for at in rows)

    def step(tb, xs):
        for i in range(SUBS):
            at = pl.ds(tb * groups * SUBS + i, groups, stride=SUBS)
            u = u_ref[at, :]
            xs = tuple(q * x + u for q, x in zip(qs, xs))
            if z_ref is not None:
                terms = [skip_ref[...] * u] + [r * x for r, x in zip(rs, xs)]
                while len(terms) > 1:
                    terms = [functools.reduce(jnp.add, terms[n:n + 2]) for n in range(0, len(terms), 2)]
                z_ref[at, :] = terms[0]
        return xs

    if first == 0:
        xs = (jnp.zeros((groups, LANES), jnp.float32),) * ORDER
    else:
        xs = tuple(x_ref[at, :] for at in rows)
    xs = lax.fori_loop(first, last, step, xs)
    for at, x in zip(rows, xs):
        x_ref[at, :] = x


def decay_of(rate, positions):
    return jnp.exp(rate * -positions)


def half_rates(rate_ref):
    half = rate_ref.shape[0] // CORES
    core = lax.axis_index("ctx") % CORES
    return pl.ds(pl.multiple_of(core * half, SUBS), half)


def chip_kernel(rate_ref, ends_ref, total_ref):
    rows = half_rates(rate_ref)
    decay = decay_of(rate_ref[rows, :], float(LANES))
    total = (decay * ends_ref[0, rows, :] + ends_ref[1, rows, :]).astype(total_ref.dtype)
    for copy in range(total_ref.shape[0]):
        total_ref[copy] = total


def prefix(part, count, decay, place):
    run = jnp.zeros(decay.shape, jnp.float32)
    before = run
    for n in range(count):
        before = jnp.where(place == n, run, before)
        run = decay * run + part(n).astype(jnp.float32)
    return before, run


def ring_kernel(rate_ref, totals_ref, u_ref, r_ref, skip_ref, z_in_ref, e_in_ref, q8_in_ref, wholes_ref, z_ref, e_ref, q8_ref, q_ref, x_ref):
    me = lax.axis_index("ctx")
    decay = decay_of(rate_ref[half_rates(rate_ref), :], float(CORES * LANES))
    before, run = prefix(lambda n: totals_ref[RING_ORDER.index(n)], RINGS, decay, me // CORES % RINGS)
    x = me // (CORES * RINGS)
    for n in range(wholes_ref.shape[0]):
        wholes_ref[n] = jnp.where(x == X_ORDER[n][0], before, run).astype(wholes_ref.dtype)

    @pl.when(defers())
    def _():
        q_ref[...] = jnp.exp(-rate_ref[...])
        tables(q_ref, r_ref, e_ref, q8_ref)
        recur(0, u_ref.shape[0] // (SUBS * SUBS), x_ref, u_ref, q_ref, r_ref, skip_ref, z_ref)


def block_start(rate_ref, wholes_ref, ends_ref, s_ref):
    me = lax.axis_index("ctx")
    x, z, core = me // (CORES * RINGS), me // CORES % RINGS, me % CORES
    half = wholes_ref.shape[1]
    for h in range(CORES):
        rows = pl.ds(h * half, half)
        rate = rate_ref[rows, :]
        far, _ = prefix(
            lambda n: wholes_ref[X_ORDER.index((n, h))], wholes_ref.shape[0] // CORES,
            decay_of(rate, float(RINGS * CORES * LANES)), x,
        )
        near = wholes_ref[X_ORDER.index((0, h))]
        for n in range(1, wholes_ref.shape[0] // CORES):
            near = jnp.where(x == n, wholes_ref[X_ORDER.index((n, h))], near)
        near = near.astype(jnp.float32)
        first = decay_of(rate, float(CORES * LANES) * z.astype(jnp.float32)) * far + near
        second = decay_of(rate, float(LANES)) * first + ends_ref[0, rows, :]
        s_ref[rows, :] = jnp.where(core == 0, first, second)


def gate_kernel(q_ref, z_ref, e_ref, q8_ref, rate_ref, wholes_ref, ends_ref, gated_ref, sums_ref, sq_ref, s_ref):
    block_start(rate_ref, wholes_ref, ends_ref, s_ref)
    tokens, width = q_ref.shape
    groups = width // LANES
    for g in range(groups):
        vs, decays = [], []
        for m in range(ORDER):
            row = pl.ds(m * groups + g, 1)
            s = jnp.broadcast_to(s_ref[row, :], (SUBS, LANES))
            vs.append(s * e_ref[pl.ds((m * groups + g) * SUBS, SUBS), :])
            decays.append(jnp.broadcast_to(q8_ref[row, :], (SUBS, LANES)))
        for pair in range(tokens // 16):
            parts = []
            for half in range(2):
                tb = 2 * pair + half
                parts.append(z_ref[pl.ds((tb * groups + g) * SUBS, SUBS), :] + functools.reduce(jnp.add, vs))
                vs = [v * d for v, d in zip(vs, decays)]
            rows, cols = pl.ds(pair * 16, 16), pl.ds(g * LANES, LANES)
            wide = q_ref[rows, cols].astype(jnp.float32) * jnp.concatenate(parts, axis=0)
            gated = wide.astype(jnp.bfloat16)
            gated_ref[rows, cols] = gated
            square = gated.astype(jnp.float32)
            square = square * square
            if g == 0:
                sq_ref[rows, :] = square
            else:
                sq_ref[rows, :] = sq_ref[rows, :] + square
    sums = jnp.sum(sq_ref[...].T, axis=0, keepdims=True)
    sums_ref[...] = jnp.broadcast_to(sums, sums_ref.shape)


def norm_kernel(scale, sums_ref, gated_ref, out_hbm, out_ref, sems):
    tokens, width = gated_ref.shape
    chunks = sems.shape[0]
    total = jnp.sum(sums_ref[...], axis=0, keepdims=True)
    inv = 1.0 / jnp.sqrt(total * scale + 1e-06)
    inv = jnp.broadcast_to(inv, (LANES, tokens)).T
    copies = []
    for chunk in range(chunks):
        size = tokens // chunks
        rows = pl.ds(chunk * size, size)
        part = inv[chunk * size:(chunk + 1) * size]
        for g in range(width // LANES):
            cols = pl.ds(g * LANES, LANES)
            out_ref[rows, cols] = (gated_ref[rows, cols].astype(jnp.float32) * part).astype(jnp.bfloat16)
        copies.append(pltpu.make_async_copy(out_ref.at[rows, :], out_hbm.at[rows, :], sems.at[chunk]))
        copies[-1].start()
    for copy in copies:
        copy.wait()


def per_device(hyena_q, hyena_k, hyena_v, filter_rate, filter_residue, skip_gain):
    n_ctx = lax.axis_size("ctx")
    n_tp = lax.axis_size("tp")
    tokens, width = hyena_q.shape
    groups = width // LANES
    f32, bf16 = jnp.float32, jnp.bfloat16
    rows = ORDER * groups
    half = rows // CORES
    shape = jax.ShapeDtypeStruct
    state = shape((rows, LANES), f32)
    table = shape((tokens * groups, LANES), f32)
    small = pltpu.VMEM((rows, LANES), f32)
    tile = pltpu.VMEM((tokens, width), bf16)
    n_x = n_ctx // (CORES * RINGS)
    pairs = [[CORES * i + c for c in range(CORES)] for i in range(n_ctx // CORES)]
    along_z = [
        [(x * RINGS + z) * CORES + c for z in RING_ORDER] for x in range(n_x) for c in range(CORES)
    ]
    along_x = [
        [(x * RINGS + z) * CORES + c for x, c in X_ORDER] for z in range(RINGS)
    ]

    def swap(array, places):
        return lax.all_to_all(
            array, "ctx", split_axis=0, concat_axis=0, tiled=True, axis_index_groups=places
        )

    rate = filter_rate.T
    weights = shape((rows * SUBS, LANES), f32)
    modes = pltpu.VMEM((ORDER, width), f32)
    ends, z, e, q8, rate_rows, u, residues, skip = call(
        state_kernel, (state, table, weights, state, state, table, state, shape((groups, LANES), f32)),
        (tile, tile, modes, modes, small,
         pltpu.SemaphoreType.DMA((2, CHUNKS)), pltpu.SemaphoreType.DMA((3,))),
        "states", (pltpu.HBM,) * 5,
    )(*(
        pltpu.with_memory_space_constraint(array, pltpu.HBM)
        for array in (hyena_k, hyena_v, rate, filter_residue.T, skip_gain.reshape(groups, LANES))
    ))
    ends = lax.all_gather(ends, "ctx", axis_index_groups=pairs)
    totals = call(chip_kernel, shape((RINGS, half, LANES), Z_TYPE), (), "chip")(rate_rows, ends)
    totals = swap(totals, along_z)
    wholes, z, e, q8 = call(
        ring_kernel, (shape((n_x * CORES, half, LANES), X_TYPE), table, weights, state), (small, small), "ring",
        aliases={5: 1, 6: 2, 7: 3},
    )(rate_rows, totals, u, residues, skip, z, e, q8)
    wholes = swap(wholes, along_x)
    gated, sums = call(
        gate_kernel,
        (shape((tokens, width), bf16), shape((n_tp, tokens), f32)),
        (pltpu.VMEM((tokens, LANES), f32), small), "gate",
    )(hyena_q, z, e, q8, rate_rows, wholes, ends)
    all_sums = lax.all_to_all(
        sums, "tp", split_axis=0, concat_axis=0, tiled=True, axis_index_groups=[TP_ORDER]
    )
    return call(
        functools.partial(norm_kernel, 1.0 / (n_tp * width)),
        shape((tokens, width), bf16), (tile, pltpu.SemaphoreType.DMA((4,))), "norm",
        (pltpu.VMEM,) * 2, pltpu.HBM,
    )(all_sums, gated)


def solution(mesh):
    in_specs = (
        P("ctx", "tp"),
        P("ctx", "tp"),
        P("ctx", "tp"),
        P("tp", None),
        P("tp", None),
        P("tp"),
    )
    return jax.shard_map(
        per_device, mesh=mesh, in_specs=in_specs, out_specs=P("ctx", "tp"), check_vma=False
    )
```

```python
import functools

import jax
import jax.numpy as jnp
from jax import lax
from jax.experimental import pallas as pl
from jax.experimental.pallas import tpu as pltpu
from jax.sharding import PartitionSpec as P

ORDER = 16
LANES = 128
SUBS = 8
CORES = 2
RINGS = 8
RING_ORDER = (6, 7, 0, 1, 2, 3, 4, 5)
TP_ORDER = [4, 5, 6, 7, 0, 1, 2, 3]
X_ORDER = ((2, 1), (0, 0), (0, 1), (1, 0), (1, 1), (2, 0), (3, 0), (3, 1))
CHUNKS = 1
Z_TYPE = jnp.bfloat16
X_TYPE = jnp.bfloat16


def call(kernel, out_shape, scratch=(), name=None, ins=None, outs=None, aliases={}):
    specs = {}
    if ins is not None:
        specs["in_specs"] = [pl.BlockSpec(memory_space=space) for space in ins]
    if outs is not None:
        specs["out_specs"] = pl.BlockSpec(memory_space=outs)
    return pl.pallas_call(
        kernel,
        out_shape=out_shape,
        scratch_shapes=scratch,
        input_output_aliases=aliases,
        name=name,
        compiler_params=pltpu.CompilerParams(vmem_limit_bytes=48 * 1024 * 1024),
        **specs,
    )


def fill_modes(src_ref, dst_ref, fn):
    groups = src_ref.shape[1] // LANES
    for g in range(groups):
        dst_ref[pl.ds(g, ORDER, stride=groups), :] = fn(src_ref[:, pl.ds(g * LANES, LANES)])


def tables(q_ref, r_ref, e_ref, q8_ref):
    groups = SUBS
    for m in range(ORDER):
        rows = pl.ds(m * groups, groups)
        q = q_ref[rows, :]
        w = r_ref[rows, :] * q
        for i in range(SUBS):
            e_ref[pl.ds(m * groups * SUBS + i, groups, stride=SUBS), :] = w
            w = w * q
        q2 = q * q
        q4 = q2 * q2
        q8_ref[rows, :] = q4 * q4


def state_kernel(
    k_hbm, v_hbm, rate_hbm, res_hbm, skip_hbm, end_ref, z_ref, e_ref, q8_ref, rate_rows_ref, u_ref, r_ref, skip_ref,
    k_ref, v_ref, rate_ref, res_ref, q_ref, sems, mode_sems,
):
    tokens, width = k_ref.shape
    groups = width // LANES
    chunks = sems.shape[1]
    size = tokens // chunks

    def fetch(chunk):
        rows = pl.ds(chunk * size, size)
        return (
            pltpu.make_async_copy(k_hbm.at[rows, :], k_ref.at[rows, :], sems.at[0, chunk]),
            pltpu.make_async_copy(v_hbm.at[rows, :], v_ref.at[rows, :], sems.at[1, chunk]),
        )

    modes = (
        pltpu.make_async_copy(rate_hbm, rate_ref, mode_sems.at[0]),
        pltpu.make_async_copy(res_hbm, res_ref, mode_sems.at[1]),
        pltpu.make_async_copy(skip_hbm, skip_ref, mode_sems.at[2]),
    )
    modes[0].start()
    for chunk in range(chunks):
        for copy in fetch(chunk):
            copy.start()
    for copy in modes[1:]:
        copy.start()
    modes[0].wait()
    fill_modes(rate_ref, rate_rows_ref, lambda r: r)
    q_ref[...] = jnp.exp(-rate_rows_ref[...])

    @pl.when(jnp.logical_not(defers()))
    def _():
        for copy in modes[1:]:
            copy.wait()
        fill_modes(res_ref, r_ref, lambda r: r)
        tables(q_ref, r_ref, e_ref, q8_ref)

    for chunk in range(chunks):
        for copy in fetch(chunk):
            copy.wait()
        for pair in range(chunk * size // 16, (chunk + 1) * size // 16):
            rows = pl.ds(pair * 16, 16)
            for g in range(groups):
                cols = pl.ds(g * LANES, LANES)
                p = k_ref[rows, cols].astype(jnp.float32) * v_ref[rows, cols].astype(jnp.float32)
                p = p.astype(jnp.bfloat16).astype(jnp.float32)
                u_ref[pl.ds((2 * pair * groups + g) * SUBS, SUBS), :] = p[:SUBS]
                u_ref[pl.ds(((2 * pair + 1) * groups + g) * SUBS, SUBS), :] = p[SUBS:]
        blocks = (chunk * size // SUBS, (chunk + 1) * size // SUBS)

        @pl.when(defers())
        def _():
            recur(*blocks, end_ref, u_ref, q_ref, None, None, None)

        @pl.when(jnp.logical_not(defers()))
        def _():
            recur(*blocks, end_ref, u_ref, q_ref, r_ref, skip_ref, z_ref)

    @pl.when(defers())
    def _():
        for copy in modes[1:]:
            copy.wait()
        fill_modes(res_ref, r_ref, lambda r: r)


def defers():
    return lax.axis_index("ctx") // CORES % RINGS >= RINGS // 2


def recur(first, last, x_ref, u_ref, q_ref, r_ref, skip_ref, z_ref):
    groups = SUBS
    rows = [pl.ds(m * groups, groups) for m in range(ORDER)]
    qs = tuple(q_ref[at, :] for at in rows)
    if z_ref is not None:
        rs = tuple(r_ref[at, :] for at in rows)

    def step(tb, xs):
        for i in range(SUBS):
            at = pl.ds(tb * groups * SUBS + i, groups, stride=SUBS)
            u = u_ref[at, :]
            xs = tuple(q * x + u for q, x in zip(qs, xs))
            if z_ref is not None:
                terms = [skip_ref[...] * u] + [r * x for r, x in zip(rs, xs)]
                while len(terms) > 1:
                    terms = [functools.reduce(jnp.add, terms[n:n + 2]) for n in range(0, len(terms), 2)]
                z_ref[at, :] = terms[0]
        return xs

    if first == 0:
        xs = (jnp.zeros((groups, LANES), jnp.float32),) * ORDER
    else:
        xs = tuple(x_ref[at, :] for at in rows)
    xs = lax.fori_loop(first, last, step, xs)
    for at, x in zip(rows, xs):
        x_ref[at, :] = x


def decay_of(rate, positions):
    return jnp.exp(rate * -positions)


def half_rates(rate_ref):
    half = rate_ref.shape[0] // CORES
    core = lax.axis_index("ctx") % CORES
    return pl.ds(pl.multiple_of(core * half, SUBS), half)


def chip_kernel(rate_ref, ends_ref, total_ref):
    rows = half_rates(rate_ref)
    decay = decay_of(rate_ref[rows, :], float(LANES))
    total = (decay * ends_ref[0, rows, :] + ends_ref[1, rows, :]).astype(total_ref.dtype)
    for copy in range(total_ref.shape[0]):
        total_ref[copy] = total


def prefix(part, count, decay, place):
    run = jnp.zeros(decay.shape, jnp.float32)
    before = run
    for n in range(count):
        before = jnp.where(place == n, run, before)
        run = decay * run + part(n).astype(jnp.float32)
    return before, run


def ring_kernel(rate_ref, totals_ref, u_ref, r_ref, skip_ref, z_in_ref, e_in_ref, q8_in_ref, wholes_ref, z_ref, e_ref, q8_ref, q_ref, x_ref):
    me = lax.axis_index("ctx")
    decay = decay_of(rate_ref[half_rates(rate_ref), :], float(CORES * LANES))
    before, run = prefix(lambda n: totals_ref[RING_ORDER.index(n)], RINGS, decay, me // CORES % RINGS)
    x = me // (CORES * RINGS)
    for n in range(wholes_ref.shape[0]):
        wholes_ref[n] = jnp.where(x == X_ORDER[n][0], before, run).astype(wholes_ref.dtype)

    @pl.when(defers())
    def _():
        q_ref[...] = jnp.exp(-rate_ref[...])
        tables(q_ref, r_ref, e_ref, q8_ref)
        recur(0, u_ref.shape[0] // (SUBS * SUBS), x_ref, u_ref, q_ref, r_ref, skip_ref, z_ref)


def block_start(rate_ref, wholes_ref, ends_ref, s_ref):
    me = lax.axis_index("ctx")
    x, z, core = me // (CORES * RINGS), me // CORES % RINGS, me % CORES
    half = wholes_ref.shape[1]
    for h in range(CORES):
        rows = pl.ds(h * half, half)
        rate = rate_ref[rows, :]
        far, _ = prefix(
            lambda n: wholes_ref[X_ORDER.index((n, h))], wholes_ref.shape[0] // CORES,
            decay_of(rate, float(RINGS * CORES * LANES)), x,
        )
        near = wholes_ref[X_ORDER.index((0, h))]
        for n in range(1, wholes_ref.shape[0] // CORES):
            near = jnp.where(x == n, wholes_ref[X_ORDER.index((n, h))], near)
        near = near.astype(jnp.float32)
        first = decay_of(rate, float(CORES * LANES) * z.astype(jnp.float32)) * far + near
        second = decay_of(rate, float(LANES)) * first + ends_ref[0, rows, :]
        s_ref[rows, :] = jnp.where(core == 0, first, second)


def gate_kernel(q_ref, z_ref, e_ref, q8_ref, rate_ref, wholes_ref, ends_ref, gated_ref, sums_ref, sq_ref, s_ref):
    block_start(rate_ref, wholes_ref, ends_ref, s_ref)
    tokens, width = q_ref.shape
    groups = width // LANES
    for g in range(groups):
        vs, decays = [], []
        for m in range(ORDER):
            row = pl.ds(m * groups + g, 1)
            s = jnp.broadcast_to(s_ref[row, :], (SUBS, LANES))
            vs.append(s * e_ref[pl.ds((m * groups + g) * SUBS, SUBS), :])
            decays.append(jnp.broadcast_to(q8_ref[row, :], (SUBS, LANES)))
        for pair in range(tokens // 16):
            parts = []
            for half in range(2):
                tb = 2 * pair + half
                parts.append(z_ref[pl.ds((tb * groups + g) * SUBS, SUBS), :] + functools.reduce(jnp.add, vs))
                vs = [v * d for v, d in zip(vs, decays)]
            rows, cols = pl.ds(pair * 16, 16), pl.ds(g * LANES, LANES)
            wide = q_ref[rows, cols].astype(jnp.float32) * jnp.concatenate(parts, axis=0)
            gated = wide.astype(jnp.bfloat16)
            gated_ref[rows, cols] = gated
            square = gated.astype(jnp.float32)
            square = square * square
            if g == 0:
                sq_ref[rows, :] = square
            else:
                sq_ref[rows, :] = sq_ref[rows, :] + square
    sums = jnp.sum(sq_ref[...].T, axis=0, keepdims=True)
    sums_ref[...] = jnp.broadcast_to(sums, sums_ref.shape)


def norm_kernel(scale, sums_ref, gated_ref, out_hbm, out_ref, sems):
    tokens, width = gated_ref.shape
    chunks = sems.shape[0]
    total = jnp.sum(sums_ref[...], axis=0, keepdims=True)
    inv = 1.0 / jnp.sqrt(total * scale + 1e-06)
    inv = jnp.broadcast_to(inv, (LANES, tokens)).T
    copies = []
    for chunk in range(chunks):
        size = tokens // chunks
        rows = pl.ds(chunk * size, size)
        part = inv[chunk * size:(chunk + 1) * size]
        for g in range(width // LANES):
            cols = pl.ds(g * LANES, LANES)
            out_ref[rows, cols] = (gated_ref[rows, cols].astype(jnp.float32) * part).astype(jnp.bfloat16)
        copies.append(pltpu.make_async_copy(out_ref.at[rows, :], out_hbm.at[rows, :], sems.at[chunk]))
        copies[-1].start()
    for copy in copies:
        copy.wait()


def per_device(hyena_q, hyena_k, hyena_v, filter_rate, filter_residue, skip_gain):
    n_ctx = lax.axis_size("ctx")
    n_tp = lax.axis_size("tp")
    tokens, width = hyena_q.shape
    groups = width // LANES
    f32, bf16 = jnp.float32, jnp.bfloat16
    rows = ORDER * groups
    half = rows // CORES
    shape = jax.ShapeDtypeStruct
    state = shape((rows, LANES), f32)
    table = shape((tokens * groups, LANES), f32)
    small = pltpu.VMEM((rows, LANES), f32)
    tile = pltpu.VMEM((tokens, width), bf16)
    n_x = n_ctx // (CORES * RINGS)
    pairs = [[CORES * i + c for c in range(CORES)] for i in range(n_ctx // CORES)]
    along_z = [
        [(x * RINGS + z) * CORES + c for z in RING_ORDER] for x in range(n_x) for c in range(CORES)
    ]
    along_x = [
        [(x * RINGS + z) * CORES + c for x, c in X_ORDER] for z in range(RINGS)
    ]

    def swap(array, places):
        return lax.all_to_all(
            array, "ctx", split_axis=0, concat_axis=0, tiled=True, axis_index_groups=places
        )

    rate = filter_rate.T
    weights = shape((rows * SUBS, LANES), f32)
    modes = pltpu.VMEM((ORDER, width), f32)
    ends, z, e, q8, rate_rows, u, residues, skip = call(
        state_kernel, (state, table, weights, state, state, table, state, shape((groups, LANES), f32)),
        (tile, tile, modes, modes, small,
         pltpu.SemaphoreType.DMA((2, CHUNKS)), pltpu.SemaphoreType.DMA((3,))),
        "states", (pltpu.HBM,) * 5,
    )(*(
        pltpu.with_memory_space_constraint(array, pltpu.HBM)
        for array in (hyena_k, hyena_v, rate, filter_residue.T, skip_gain.reshape(groups, LANES))
    ))
    ends = lax.all_gather(ends, "ctx", axis_index_groups=pairs)
    totals = call(chip_kernel, shape((RINGS, half, LANES), Z_TYPE), (), "chip")(rate_rows, ends)
    totals = swap(totals, along_z)
    wholes, z, e, q8 = call(
        ring_kernel, (shape((n_x * CORES, half, LANES), X_TYPE), table, weights, state), (small, small), "ring",
        aliases={5: 1, 6: 2, 7: 3},
    )(rate_rows, totals, u, residues, skip, z, e, q8)
    wholes = swap(wholes, along_x)
    gated, sums = call(
        gate_kernel,
        (shape((tokens, width), bf16), shape((n_tp, tokens), f32)),
        (pltpu.VMEM((tokens, LANES), f32), small), "gate",
    )(hyena_q, z, e, q8, rate_rows, wholes, ends)
    all_sums = lax.all_to_all(
        sums, "tp", split_axis=0, concat_axis=0, tiled=True, axis_index_groups=[TP_ORDER]
    )
    return call(
        functools.partial(norm_kernel, 1.0 / (n_tp * width)),
        shape((tokens, width), bf16), (tile, pltpu.SemaphoreType.DMA((4,))), "norm",
        (pltpu.VMEM,) * 2, pltpu.HBM,
    )(all_sums, gated)


def solution(mesh):
    in_specs = (
        P("ctx", "tp"),
        P("ctx", "tp"),
        P("ctx", "tp"),
        P("tp", None),
        P("tp", None),
        P("tp"),
    )
    return jax.shard_map(
        per_device, mesh=mesh, in_specs=in_specs, out_specs=P("ctx", "tp"), check_vma=False
    )
```
